32 devices in a mesh: row: 8 (over y, x, core), col: 4 (over z).
Axes of the slice: x: 2, y: 2, z: 4, core: 2. Of those that a mesh axis runs over, the one named last changes fastest.
Arguments:
- mixture_fractions: float32 [54, 64, 512], P(None, 'row', 'col'), may hold values from -6 to 6
- spreading_coefficient: float32 [64, 512], P('row', 'col'), may hold values from 0.02 to 0.12
- flow_speed_vector: float32 [2, 64, 512], P(None, 'row', 'col'), may hold values from -0.15 to 0.15
- thermal_state: float32 [64, 512], P('row', 'col'), may hold values from -6 to 6
- chemistry_active_indicator: int32 [64, 512], P('row', 'col'), may hold values from 0 to 1, as said below
- entry_level_matrix: bfloat16 [256, 55], replicated, may hold values from -0.875 to 0.875
- entry_level_offset: float32 [256], replicated, may hold values from -3 to 3
- hidden_level_matrix: bfloat16 [256, 256], replicated, may hold values from -0.375 to 0.375
- hidden_level_offset: float32 [256], replicated, may hold values from -3 to 3
- final_level_matrix: bfloat16 [54, 256], replicated, may hold values from -0.375 to 0.375
- final_level_offset: float32 [54], replicated, may hold values from -3 to 3
Outputs:
- species_next: float32 [54, 64, 512], P(None, 'row', 'col')
The draws below stay inside these ranges and needn't reach their ends.
Inputs may be any that keep to these rules, and one draw needn't show every extreme that they name: `chemistry_active_indicator`: split the grid into tiles of 8 x 128 cells and bands of 8 rows. Every tile holds at most 384 flagged cells, and in every band some tile holds exactly 384; every band holds exactly 512 flagged cells.
All inputs are finite; a program needn't handle non-finite values.
Results may differ from the reference program's by a relative error of at most 0.0003.
Values sent between devices are 32-bit elements; how exact they have to be, the bound alone decides.
A program may use at most 64 MiB of HBM per device.

```python
import math
import jax
import jax.numpy as jnp
from jax import lax

CHEMICAL_KINDS = 54
HID = 256
SUBSTEPS = 8
TRANSPORT_STEPS = 3
CY = 8
CX = 128
MESH_HEIGHT = 64
MESH_WIDTH = 512
ROW_SHARE = 128
N_ROW = 8
N_COL = 4


def draw_chemistry_active_indicator(key, part):
    first_key, second_key, third_key = jax.random.split(key, 3)
    share_cells = CY * CX // 8
    cell_capacity = 3 * share_cells
    cell_total = CY * CX
    remainder = N_COL * share_cells - cell_capacity
    weights = jax.random.randint(first_key, (N_ROW, N_COL), 2, 6)
    busiest = jax.random.randint(second_key, (N_ROW,), 0, N_COL)
    holds_most_work = jnp.arange(N_COL)[None, :] == busiest[:, None]
    weights = jnp.where(holds_most_work, 0, weights)
    lowest_share = remainder * weights // jnp.sum(weights, axis=1, keepdims=True)
    leftover_cells = remainder - jnp.sum(lowest_share, axis=1, keepdims=True)
    drawn_position = jnp.cumsum(jnp.where(holds_most_work, 0, 1), axis=1) - 1
    extra_cell = jnp.where(jnp.logical_and(jnp.logical_not(holds_most_work), drawn_position < leftover_cells), 1, 0)
    flagged_counts = jnp.where(holds_most_work, cell_capacity, lowest_share + extra_cell).reshape(-1, 1)
    subkeys = jax.random.split(third_key, N_ROW * N_COL)
    orders = jax.vmap(lambda single: jax.random.permutation(single, cell_total))(subkeys)
    active = (orders < flagged_counts).astype(jnp.int32)
    active = active.reshape(N_ROW, N_COL, CY, CX).transpose(0, 2, 1, 3)
    return active.reshape(CY * N_ROW, CX * N_COL)


def level_of(stream_key, shape, pieces, low, high):
    level = 1.0
    for dim, parts in pieces:
        steps = jax.random.uniform(jax.random.fold_in(jax.random.fold_in(stream_key, 6), dim), (parts,), jnp.float32, low / len(pieces), high / len(pieces))
        level = level * jnp.repeat(jnp.exp(steps), shape[dim] // parts).reshape((-1,) + (1,) * (len(shape) - 1 - dim))
    return level


def noise(rng, shape, width, limit, cuts=(), kind=jnp.bfloat16):
    values = width * jax.random.normal(rng, shape, jnp.float32)
    if cuts:
        values = values * level_of(rng, shape, cuts, -0.22, 0.18)
    return jnp.clip(values, -limit, limit).astype(kind)


def setup_inputs(seed: int = 0) -> dict:
    key_list = jax.random.split(jax.random.key(seed), 12)
    mixture_fractions = noise(key_list[0], (CHEMICAL_KINDS, MESH_HEIGHT, MESH_WIDTH), 1.0, 6.0, ((1, 8), (2, 4)), jnp.float32)
    spreading_coefficient = jnp.clip(jnp.exp(math.log(0.12) - 1.7917595 * jax.random.uniform(key_list[1], (MESH_HEIGHT, MESH_WIDTH), jnp.float32) ** level_of(key_list[1], (MESH_HEIGHT, MESH_WIDTH), ((0, 8), (1, 4)), -0.2, 0.2)), 0.02, 0.12)
    flow_speed_vector = jnp.clip(jax.random.uniform(key_list[2], (2, MESH_HEIGHT, MESH_WIDTH), jnp.float32, -0.15, 0.15) * level_of(key_list[2], (2, MESH_HEIGHT, MESH_WIDTH), ((1, 8), (2, 4)), -0.4, 0.0), -0.15, 0.15)
    thermal_state = noise(key_list[3], (MESH_HEIGHT, MESH_WIDTH), 1.0, 6.0, ((0, 8), (1, 4)), jnp.float32)
    chemistry_active_indicator = draw_chemistry_active_indicator(jax.random.fold_in(key_list[11], 71), 0)
    entry_level_matrix = noise(key_list[5], (HID, CHEMICAL_KINDS + 1), (CHEMICAL_KINDS + 1) ** -0.5, 0.875)
    entry_level_offset = noise(key_list[6], (HID,), 0.5, 3.0, (), jnp.float32)
    hidden_level_matrix = noise(key_list[7], (HID, HID), HID ** -0.5, 0.375)
    hidden_level_offset = noise(key_list[8], (HID,), 0.5, 3.0, (), jnp.float32)
    final_level_matrix = noise(key_list[9], (CHEMICAL_KINDS, HID), HID ** -0.5, 0.375)
    final_level_offset = noise(key_list[10], (CHEMICAL_KINDS,), 0.5, 3.0, (), jnp.float32)
    return {"mixture_fractions": mixture_fractions, "spreading_coefficient": spreading_coefficient, "flow_speed_vector": flow_speed_vector, "thermal_state": thermal_state, "chemistry_active_indicator": chemistry_active_indicator, "entry_level_matrix": entry_level_matrix, "entry_level_offset": entry_level_offset, "hidden_level_matrix": hidden_level_matrix, "hidden_level_offset": hidden_level_offset, "final_level_matrix": final_level_matrix, "final_level_offset": final_level_offset}


time_step = 1.0
chem_step = 0.0625


def advance(padded, pad_diff, speed_cols, speed_rows):
    left_vals = padded[..., 1:-1, :-1]
    right_vals = padded[..., 1:-1, 1:]
    face_diff = 0.5 * (pad_diff[1:-1, :-1] + pad_diff[1:-1, 1:])
    face_speed = 0.5 * (speed_cols[1:-1, :-1] + speed_cols[1:-1, 1:])
    flux_cols = face_diff * (right_vals - left_vals) - (jnp.maximum(face_speed, 0.0) * left_vals + jnp.minimum(face_speed, 0.0) * right_vals)
    lower_vals = padded[..., :-1, 1:-1]
    upper_vals = padded[..., 1:, 1:-1]
    face_diff = 0.5 * (pad_diff[:-1, 1:-1] + pad_diff[1:, 1:-1])
    face_speed = 0.5 * (speed_rows[:-1, 1:-1] + speed_rows[1:, 1:-1])
    flux_rows = face_diff * (upper_vals - lower_vals) - (jnp.maximum(face_speed, 0.0) * lower_vals + jnp.minimum(face_speed, 0.0) * upper_vals)
    change = flux_cols[..., 1:] - flux_cols[..., :-1] + flux_rows[..., 1:, :] - flux_rows[..., :-1, :]
    return padded[..., 1:-1, 1:-1] + time_step * change


def network(inputs, entry_level_matrix, entry_level_offset, hidden_level_matrix, hidden_level_offset, final_level_matrix, final_level_offset):
    hidden = jnp.tanh(jnp.dot(entry_level_matrix, inputs, preferred_element_type=jnp.float32) + entry_level_offset[:, None]).astype(jnp.bfloat16)
    hidden = jnp.tanh(jnp.dot(hidden_level_matrix, hidden, preferred_element_type=jnp.float32) + hidden_level_offset[:, None]).astype(jnp.bfloat16)
    return jnp.dot(final_level_matrix, hidden, preferred_element_type=jnp.float32) + final_level_offset[:, None]


def integrate(state, heat, entry_level_matrix, entry_level_offset, hidden_level_matrix, hidden_level_offset, final_level_matrix, final_level_offset):
    total = jnp.zeros(state.shape, jnp.float32)
    for index in range(SUBSTEPS):
        inputs = jnp.concatenate([state + chem_step * total, heat[None]], 0).astype(jnp.bfloat16)
        total = total + network(inputs, entry_level_matrix, entry_level_offset, hidden_level_matrix, hidden_level_offset, final_level_matrix, final_level_offset)
    return chem_step * total


def reference(mixture_fractions, spreading_coefficient, flow_speed_vector, thermal_state, chemistry_active_indicator, entry_level_matrix, entry_level_offset, hidden_level_matrix, hidden_level_offset, final_level_matrix, final_level_offset):
    pad_diff = jnp.pad(spreading_coefficient, 1)
    pad_speed = jnp.pad(flow_speed_vector, ((0, 0), (1, 1), (1, 1)))
    carried_quantity = mixture_fractions
    for section in range(TRANSPORT_STEPS):
        carried_quantity = lax.map(lambda field: advance(jnp.pad(field, 1), pad_diff, pad_speed[0], pad_speed[1]), carried_quantity)
    predictor_vector = jnp.concatenate([carried_quantity, thermal_state[None]], 0).reshape(CHEMICAL_KINDS + 1, MESH_HEIGHT * MESH_WIDTH)
    cell_total = MESH_HEIGHT * MESH_WIDTH
    chosen = jnp.nonzero(chemistry_active_indicator.reshape(-1), size=cell_total // 8, fill_value=cell_total)[0].astype(jnp.int32)
    blocks = chosen.reshape(-1, ROW_SHARE)

    def per_block(cells_here):
        inputs = jnp.take(predictor_vector, cells_here, axis=1, mode="fill", fill_value=0)
        return integrate(inputs[:CHEMICAL_KINDS], inputs[CHEMICAL_KINDS], entry_level_matrix, entry_level_offset, hidden_level_matrix, hidden_level_offset, final_level_matrix, final_level_offset)

    rates = lax.map(per_block, blocks)
    rates = jnp.transpose(rates, (1, 0, 2)).reshape(CHEMICAL_KINDS, -1)
    increments = jnp.zeros((CHEMICAL_KINDS, cell_total + 1), jnp.float32).at[:, chosen].add(rates)[:, :cell_total]
    return (carried_quantity.reshape(CHEMICAL_KINDS, cell_total) + increments).reshape(CHEMICAL_KINDS, MESH_HEIGHT, MESH_WIDTH)
```

```python
import functools

import jax
import jax.numpy as jnp
from jax import lax
from jax.experimental import pallas as pl
from jax.experimental.pallas import tpu as pltpu
from jax.sharding import PartitionSpec as P

SUBSTEPS = 8
TRANSPORT_STEPS = 3
CHEM_STEP = 0.0625
GROUP = 4
SLOT = 8
CHUNKS = 4
MESH_ID = pl.DeviceIdType.MESH
DIRECTIONS = tuple((dr, dc) for dr in (-1, 0, 1) for dc in (-1, 0, 1) if (dr, dc) != (0, 0))


def roll_lanes(x, shift):
    return pltpu.roll(x, shift % x.shape[-1], x.ndim - 1)


def roll_rows(x, shift):
    return pltpu.roll(x, shift % x.shape[-2], x.ndim - 2)


def around_rows(centre, outer, first, last):
    cu, hu = roll_rows(centre, -1), roll_rows(outer, -1)
    cd, hd = roll_rows(centre, 1), roll_rows(outer, 1)
    return (
        jnp.where(last, hu, cu),
        jnp.where(first, hd, cd),
        jnp.where(last, cu, hu),
        jnp.where(first, cd, hd),
    )


def coefficients(d, u, v, de, dw, dn, ds, ue, uw, vn, vs):
    de, dw, dn, ds = (0.5 * (d + x) for x in (de, dw, dn, ds))
    ue, uw, vn, vs = 0.5 * (u + ue), 0.5 * (u + uw), 0.5 * (v + vn), 0.5 * (v + vs)
    own = (
        1.0
        - (de + jnp.maximum(ue, 0.0))
        - (dw - jnp.minimum(uw, 0.0))
        - (dn + jnp.maximum(vn, 0.0))
        - (ds - jnp.minimum(vs, 0.0))
    )
    return (
        own,
        de - jnp.minimum(ue, 0.0),
        dw + jnp.maximum(uw, 0.0),
        dn - jnp.minimum(vn, 0.0),
        ds + jnp.maximum(vs, 0.0),
    )


def apply_step(w, own, east, west, north, south):
    return w[0] * own + w[1] * east + w[2] * west + w[3] * north + w[4] * south


def kernel(
    rows, cols, species,
    mix_hbm, diff_hbm, speed_hbm, heat_hbm, active_hbm, w1_hbm, w2_hbm, w3_hbm,
    b1_ref, b2_ref, b3_ref,
    out_ref,
    field, halo, side, corner, next_c, next_h, adv, heat_v, active_v, w1_v, w2_v, w3_v, w1_p, w3_p, b3_p,
    local_sem, send_sem, recv_sem,
):
    r, c = lax.axis_index("row"), lax.axis_index("col")
    padded = pl.cdiv(species, GROUP) * GROUP
    slots = padded // GROUP
    coef = padded
    packed = padded + GROUP

    loads = [
        pltpu.make_async_copy(mix_hbm, field.at[pl.ds(0, species)], local_sem.at[0]),
        pltpu.make_async_copy(diff_hbm, field.at[coef], local_sem.at[1]),
        pltpu.make_async_copy(speed_hbm, field.at[pl.ds(coef + 1, 2)], local_sem.at[2]),
        pltpu.make_async_copy(heat_hbm, heat_v, local_sem.at[3]),
        pltpu.make_async_copy(active_hbm, active_v, local_sem.at[4]),
        pltpu.make_async_copy(w1_hbm, w1_v, local_sem.at[5]),
        pltpu.make_async_copy(w2_hbm, w2_v, local_sem.at[6]),
        pltpu.make_async_copy(w3_hbm, w3_v, local_sem.at[7]),
    ]
    for load in loads:
        load.start()
    halo[...] = jnp.zeros_like(halo)
    side[...] = jnp.zeros_like(side)
    corner[...] = jnp.zeros_like(corner)

    def there(dr, dc):
        ok = jnp.bool_(True)
        if dr:
            ok = jnp.logical_and(ok, r + dr < rows if dr > 0 else r + dr >= 0)
        if dc:
            ok = jnp.logical_and(ok, c + dc < cols if dc > 0 else c + dc >= 0)
        return ok

    barrier = pltpu.get_barrier_semaphore()
    for dr, dc in DIRECTIONS:
        @pl.when(there(dr, dc))
        def _(dr=dr, dc=dc):
            pl.semaphore_signal(barrier, inc=1, device_id=(r + dr, c + dc), device_id_type=MESH_ID)

    for s in [*range(species, padded), coef + 3]:
        field[s] = jnp.zeros(field.shape[1:], jnp.float32)
    lane = lax.broadcasted_iota(jnp.int32, (8, 128), 1)
    row = lax.broadcasted_iota(jnp.int32, (8, 128), 0)
    first, last = row == 0, row == 7
    west_end, east_end = lane == 0, lane == 127
    in_slot = lane % SLOT
    slot = lane // SLOT
    for load in loads[:3]:
        load.wait()
    pack = jnp.zeros((GROUP, 8, 128), jnp.float32)
    for k in range(slots + 1):
        pack = jnp.where(slot == k, roll_lanes(field[pl.ds(GROUP * k, GROUP)], SLOT * k + 3), pack)
    field[pl.ds(packed, GROUP)] = pack

    one = lambda ok: jnp.where(ok, 1, 0)
    row_sides, col_sides = one(r > 0) + one(r < rows - 1), one(c > 0) + one(c < cols - 1)
    pl.semaphore_wait(barrier, (1 + row_sides) * (1 + col_sides) - 1)

    def message(index):
        dr, dc = DIRECTIONS[index]
        strip = {1: pl.ds(5, 3), -1: pl.ds(0, 3), 0: pl.ds(0, 8)}[dr]
        if dc == 0:
            src, dst = field.at[:, strip, :], halo.at[:, strip, :]
        else:
            target = side if dr == 0 else corner
            src = field.at[pl.ds(packed, GROUP), strip, :]
            dst = target.at[pl.ds(0 if dc > 0 else GROUP, GROUP), strip, :]
        return pltpu.make_async_remote_copy(
            src_ref=src, dst_ref=dst, send_sem=send_sem.at[index], recv_sem=recv_sem.at[index],
            device_id=(r + dr, c + dc), device_id_type=MESH_ID,
        )

    for index, (dr, dc) in enumerate(DIRECTIONS):
        @pl.when(there(dr, dc))
        def _(index=index):
            message(index).start()

    for load in loads[3:]:
        load.wait()
    w1_p[...] = jnp.zeros_like(w1_p)
    w1_p[pl.ds(0, species + 1), :] = w1_v[...]
    first_matrix = jnp.transpose(w1_p[...].astype(jnp.float32)).astype(jnp.bfloat16)
    w3_p[...] = jnp.zeros_like(w3_p)
    w3_p[pl.ds(0, species), :] = w3_v[...]
    hidden = w1_v.shape[1]
    bias1 = jnp.transpose(jnp.broadcast_to(b1_ref[...], (128, hidden)))
    bias2 = jnp.transpose(jnp.broadcast_to(b2_ref[...], (128, hidden)))
    b3_p[...] = jnp.zeros_like(b3_p)
    b3_p[:, pl.ds(0, species)] = b3_ref[...]
    bias3 = jnp.transpose(jnp.broadcast_to(b3_p[...], (128, 128)))[:64]

    for index, (dr, dc) in enumerate(DIRECTIONS):
        @pl.when(there(-dr, -dc))
        def _(index=index):
            message(index).wait_recv()

    own_c, own_h = field[pl.ds(packed, GROUP)], halo[pl.ds(packed, GROUP)]
    lower = in_slot < 3
    faces = [
        (jnp.where(lower, side[:GROUP], own_c), jnp.where(lower, corner[:GROUP], own_h)),
        (jnp.where(lower, own_c, side[GROUP:]), jnp.where(lower, own_h, corner[GROUP:])),
    ]
    in_outer = jnp.where(row < 4, jnp.where(r < rows - 1, 1.0, 0.0), jnp.where(r > 0, 1.0, 0.0))
    in_left = jnp.where(lower, jnp.where(c > 0, 1.0, 0.0), 1.0)
    in_right = jnp.where(lower, 1.0, jnp.where(c < cols - 1, 1.0, 0.0))

    def joined(left, right):
        return jnp.where(in_slot == 7, roll_lanes(right, -4), roll_lanes(left, -2))

    def around_lanes(x, join, k):
        moved = roll_lanes(join, -SLOT * k)
        return jnp.where(east_end, moved, roll_lanes(x, -1)), jnp.where(west_end, moved, roll_lanes(x, 1))

    def replicate(x):
        x = jnp.where(slot == slots, x, 0.0)
        for step in (8, 16, 32, 64):
            x = x + roll_lanes(x, step)
        return x

    def weights(dc_, uc, vc, dh, uh, vh, lanes_c, lanes_h, mask_c, mask_h):
        dnc, dsc, dnh, dsh = around_rows(dc_, dh, first, last)
        vnc, vsc, vnh, vsh = around_rows(vc, vh, first, last)
        (dec, dwc), (uec, uwc) = lanes_c
        (deh, dwh), (ueh, uwh) = lanes_h
        wc = coefficients(dc_, uc, vc, dec, dwc, dnc, dsc, uec, uwc, vnc, vsc)
        wh = coefficients(dh, uh, vh, deh, dwh, dnh, dsh, ueh, uwh, vnh, vsh)
        if mask_c is not None:
            wc = tuple(w * mask_c for w in wc)
        return wc, tuple(w * mask_h for w in wh)

    face_w = []
    for (fc, fh), mask in zip(faces, (in_left, in_right)):
        dc_, uc, vc = (replicate(fc[i]) for i in range(3))
        dh, uh, vh = (replicate(fh[i]) for i in range(3))
        pair = lambda x: (roll_lanes(x, -1), roll_lanes(x, 1))
        face_w.append(weights(dc_, uc, vc, dh, uh, vh, (pair(dc_), pair(uc)), (pair(dh), pair(uh)), mask, mask * in_outer))
    join_c, join_h = joined(faces[0][0], faces[1][0]), joined(faces[0][1], faces[1][1])
    tile_c, tile_h = field[pl.ds(coef, 3)], halo[pl.ds(coef, 3)]
    lanes_c = tuple(around_lanes(tile_c[i], join_c[i], slots) for i in range(2))
    lanes_h = tuple(around_lanes(tile_h[i], join_h[i], slots) for i in range(2))
    wc, wh = weights(*(tile_c[i] for i in range(3)), *(tile_h[i] for i in range(3)), lanes_c, lanes_h, None, in_outer)

    for step in range(TRANSPORT_STEPS):
        final = step == TRANSPORT_STEPS - 1
        for k in range(slots):
            here = pl.ds(GROUP * k, GROUP)
            xc, xh = (field[here], halo[here]) if step == 0 else (next_c[here], next_h[here])
            nc, sc, nh, sh = around_rows(xc, xh, first, last)
            ec, wcc = around_lanes(xc, join_c, k)
            new = apply_step(wc, xc, ec, wcc, nc, sc)
            if final:
                adv[here] = new
            else:
                eh, whh = around_lanes(xh, join_h, k)
                next_c[here] = new
                next_h[here] = apply_step(wh, xh, eh, whh, nh, sh)
        if not final:
            moved = []
            for (fc, fh), (fwc, fwh) in zip(faces, face_w):
                nc, sc, nh, sh = around_rows(fc, fh, first, last)
                moved.append((
                    apply_step(fwc, fc, roll_lanes(fc, -1), roll_lanes(fc, 1), nc, sc),
                    apply_step(fwh, fh, roll_lanes(fh, -1), roll_lanes(fh, 1), nh, sh),
                ))
            faces = moved
            join_c, join_h = joined(faces[0][0], faces[1][0]), joined(faces[0][1], faces[1][1])

    adv[species] = heat_v[...]
    for s in range(species + 1, adv.shape[0]):
        adv[s] = jnp.zeros(adv.shape[1:], jnp.float32)
    per = 8 // CHUNKS
    bases = [
        jnp.concatenate([adv[:, per * i + j, :] for j in range(per)], axis=1) for i in range(CHUNKS)
    ]
    wide = lambda b: jnp.concatenate([b] * per, axis=1)
    wide1, wide2, wide3 = wide(bias1), wide(bias2), wide(bias3)

    def substep(_, totals):
        new = []
        for base, total in zip(bases, totals):
            x = (base + CHEM_STEP * total).astype(jnp.bfloat16)
            h = jnp.dot(first_matrix, x, preferred_element_type=jnp.float32)
            h = jnp.tanh(h + wide1).astype(jnp.bfloat16)
            h = jnp.dot(w2_v[...], h, preferred_element_type=jnp.float32)
            h = jnp.tanh(h + wide2).astype(jnp.bfloat16)
            new.append(total + (jnp.dot(w3_p[...], h, preferred_element_type=jnp.float32) + wide3))
        return tuple(new)

    totals = lax.fori_loop(0, SUBSTEPS, substep, tuple(jnp.zeros_like(b) for b in bases))
    scale = CHEM_STEP * active_v[...].astype(jnp.float32)
    for i in range(CHUNKS):
        for j in range(per):
            q = per * i + j
            total = totals[i][:, 128 * j : 128 * (j + 1)]
            out_ref[:, q, :] = (adv[:, q, :] + scale[q : q + 1] * total)[:species]

    for index, (dr, dc) in enumerate(DIRECTIONS):
        @pl.when(there(dr, dc))
        def _(index=index):
            message(index).wait_send()


def shards(rows, cols, mix, diff, speed, heat, active, w1, b1, w2, b2, w3, b3):
    species, height, width = mix.shape
    padded = pl.cdiv(species, GROUP) * GROUP
    fields = padded + 2 * GROUP
    hidden, features = w1.shape
    vm = pltpu.VMEM
    f32, bf16 = jnp.float32, jnp.bfloat16
    return pl.pallas_call(
        functools.partial(kernel, rows, cols, species),
        out_shape=jax.ShapeDtypeStruct(mix.shape, mix.dtype),
        in_specs=[pl.BlockSpec(memory_space=pl.ANY)] * 8 + [pl.BlockSpec(memory_space=vm)] * 3,
        out_specs=pl.BlockSpec(memory_space=vm),
        scratch_shapes=[
            vm((fields, height, width), f32),
            vm((fields, height, width), f32),
            vm((2 * GROUP, height, width), f32),
            vm((2 * GROUP, height, width), f32),
            vm((padded, height, width), f32),
            vm((padded, height, width), f32),
            vm((64, height, width), f32),
            vm((height, width), f32),
            vm((height, width), jnp.int32),
            vm((features, hidden), bf16),
            vm(w2.shape, bf16),
            vm(w3.shape, bf16),
            vm((64, hidden), bf16),
            vm((64, hidden), bf16),
            vm((1, 128), f32),
            pltpu.SemaphoreType.DMA((8,)),
            pltpu.SemaphoreType.DMA((8,)),
            pltpu.SemaphoreType.DMA((8,)),
        ],
        compiler_params=pltpu.CompilerParams(collective_id=0, has_side_effects=True),
    )(mix, diff, speed, heat, active, w1.T, w2, w3,
      b1[None], b2[None], b3[None])


def solution(mesh):
    tile = P(None, "row", "col")
    plane = P("row", "col")
    return jax.shard_map(
        functools.partial(shards, mesh.shape["row"], mesh.shape["col"]),
        mesh=mesh,
        in_specs=(tile, plane, tile, plane, plane, P(), P(), P(), P(), P(), P()),
        out_specs=tile,
        check_vma=False,
    )
```

```python
import functools

import jax
import jax.numpy as jnp
from jax import lax
from jax.experimental import pallas as pl
from jax.experimental.pallas import tpu as pltpu
from jax.sharding import PartitionSpec as P

SUBSTEPS = 8
TRANSPORT_STEPS = 3
CHEM_STEP = 0.0625
GROUP = 4
SLOT = 8
CHUNKS = 2
WIDTH = 64
UNROLL = 1
MESH_ID = pl.DeviceIdType.MESH
DIRECTIONS = tuple((dr, dc) for dr in (-1, 0, 1) for dc in (-1, 0, 1) if (dr, dc) != (0, 0))


def roll_lanes(x, shift):
    return pltpu.roll(x, shift % x.shape[-1], x.ndim - 1)


def roll_rows(x, shift):
    return pltpu.roll(x, shift % x.shape[-2], x.ndim - 2)


def around_rows(centre, outer, first, last):
    cu, hu = roll_rows(centre, -1), roll_rows(outer, -1)
    cd, hd = roll_rows(centre, 1), roll_rows(outer, 1)
    return (
        jnp.where(last, hu, cu),
        jnp.where(first, hd, cd),
        jnp.where(last, cu, hu),
        jnp.where(first, cd, hd),
    )


def coefficients(d, u, v, de, dw, dn, ds, ue, uw, vn, vs):
    de, dw, dn, ds = (0.5 * (d + x) for x in (de, dw, dn, ds))
    ue, uw, vn, vs = 0.5 * (u + ue), 0.5 * (u + uw), 0.5 * (v + vn), 0.5 * (v + vs)
    own = (
        1.0
        - (de + jnp.maximum(ue, 0.0))
        - (dw - jnp.minimum(uw, 0.0))
        - (dn + jnp.maximum(vn, 0.0))
        - (ds - jnp.minimum(vs, 0.0))
    )
    return (
        own,
        de - jnp.minimum(ue, 0.0),
        dw + jnp.maximum(uw, 0.0),
        dn - jnp.minimum(vn, 0.0),
        ds + jnp.maximum(vs, 0.0),
    )


def apply_step(w, own, east, west, north, south):
    return w[0] * own + w[1] * east + w[2] * west + w[3] * north + w[4] * south


def kernel(
    rows, cols, species,
    mix_hbm, diff_hbm, speed_hbm, heat_hbm, active_hbm, w1_hbm, w2_hbm, w3_hbm,
    b1_ref, b2_ref, b3_ref,
    out_ref,
    field, halo, side, corner, next_c, next_h, adv, heat_v, active_v, w1_v, w2_v, w3_v, w1_p, w2_p, w3_s, w3_p, b3_p, chosen, spread,
    local_sem, send_sem, recv_sem,
):
    r, c = lax.axis_index("row"), lax.axis_index("col")
    padded = pl.cdiv(species, GROUP) * GROUP
    slots = padded // GROUP
    coef = padded
    packed = padded + GROUP

    loads = [
        pltpu.make_async_copy(mix_hbm, field.at[pl.ds(0, species)], local_sem.at[0]),
        pltpu.make_async_copy(diff_hbm, field.at[coef], local_sem.at[1]),
        pltpu.make_async_copy(speed_hbm, field.at[pl.ds(coef + 1, 2)], local_sem.at[2]),
        pltpu.make_async_copy(heat_hbm, heat_v, local_sem.at[3]),
        pltpu.make_async_copy(active_hbm, active_v, local_sem.at[4]),
        pltpu.make_async_copy(w1_hbm, w1_v, local_sem.at[5]),
        pltpu.make_async_copy(w2_hbm, w2_v, local_sem.at[6]),
        pltpu.make_async_copy(w3_hbm, w3_v, local_sem.at[7]),
    ]
    for load in loads:
        load.start()
    halo[...] = jnp.zeros_like(halo)
    side[...] = jnp.zeros_like(side)
    corner[...] = jnp.zeros_like(corner)

    def there(dr, dc):
        ok = jnp.bool_(True)
        if dr:
            ok = jnp.logical_and(ok, r + dr < rows if dr > 0 else r + dr >= 0)
        if dc:
            ok = jnp.logical_and(ok, c + dc < cols if dc > 0 else c + dc >= 0)
        return ok

    barrier = pltpu.get_barrier_semaphore()
    for dr, dc in DIRECTIONS:
        @pl.when(there(dr, dc))
        def _(dr=dr, dc=dc):
            pl.semaphore_signal(barrier, inc=1, device_id=(r + dr, c + dc), device_id_type=MESH_ID)

    for s in [*range(species, padded), coef + 3]:
        field[s] = jnp.zeros(field.shape[1:], jnp.float32)
    lane = lax.broadcasted_iota(jnp.int32, (8, 128), 1)
    row = lax.broadcasted_iota(jnp.int32, (8, 128), 0)
    first, last = row == 0, row == 7
    west_end, east_end = lane == 0, lane == 127
    in_slot = lane % SLOT
    slot = lane // SLOT
    for load in loads[:3]:
        load.wait()
    pack = jnp.zeros((GROUP, 8, 128), jnp.float32)
    for k in range(slots + 1):
        pack = jnp.where(slot == k, roll_lanes(field[pl.ds(GROUP * k, GROUP)], SLOT * k + 3), pack)
    field[pl.ds(packed, GROUP)] = pack

    one = lambda ok: jnp.where(ok, 1, 0)
    row_sides, col_sides = one(r > 0) + one(r < rows - 1), one(c > 0) + one(c < cols - 1)
    pl.semaphore_wait(barrier, (1 + row_sides) * (1 + col_sides) - 1)

    def message(index):
        dr, dc = DIRECTIONS[index]
        strip = {1: pl.ds(5, 3), -1: pl.ds(0, 3), 0: pl.ds(0, 8)}[dr]
        if dc == 0:
            src, dst = field.at[:, strip, :], halo.at[:, strip, :]
        else:
            target = side if dr == 0 else corner
            src = field.at[pl.ds(packed, GROUP), strip, :]
            dst = target.at[pl.ds(0 if dc > 0 else GROUP, GROUP), strip, :]
        return pltpu.make_async_remote_copy(
            src_ref=src, dst_ref=dst, send_sem=send_sem.at[index], recv_sem=recv_sem.at[index],
            device_id=(r + dr, c + dc), device_id_type=MESH_ID,
        )

    for index, (dr, dc) in enumerate(DIRECTIONS):
        @pl.when(there(dr, dc))
        def _(index=index):
            message(index).start()

    for load in loads[3:]:
        load.wait()
    w1_p[...] = jnp.zeros_like(w1_p)
    w1_p[pl.ds(0, species + 1), :] = w1_v[...]
    w2_p[...] = jnp.transpose(w2_v[...].astype(jnp.float32)).astype(jnp.bfloat16)
    w3_s[...] = jnp.zeros_like(w3_s)
    w3_s[pl.ds(0, species), :] = w3_v[...]
    w3_p[...] = jnp.transpose(w3_s[...].astype(jnp.float32)).astype(jnp.bfloat16)
    b3_p[...] = jnp.zeros_like(b3_p)
    b3_p[:, pl.ds(0, species)] = b3_ref[...]

    capacity = chosen.shape[0]
    flags = jnp.where(active_v[...] == 1, 1.0, 0.0)
    upto = lax.broadcasted_iota(jnp.int32, (128, 128), 0) <= lax.broadcasted_iota(jnp.int32, (128, 128), 1)
    upto = jnp.where(upto, 1.0, 0.0).astype(jnp.bfloat16)
    within = jnp.dot(flags.astype(jnp.bfloat16), upto, preferred_element_type=jnp.float32)
    offset = jnp.dot(flags.astype(jnp.bfloat16), jnp.ones((128, 128), jnp.bfloat16), preferred_element_type=jnp.float32)
    offset = jnp.where(row >= 1, roll_rows(offset, 1), 0.0)
    for shift in (1, 2, 4):
        offset = offset + jnp.where(row >= shift, roll_rows(offset, shift), 0.0)
    place = jnp.where(flags > 0.0, within + offset - 1.0, -1.0)
    index = lax.broadcasted_iota(jnp.int32, (capacity, 128), 0).astype(jnp.float32)
    for q in range(8):
        hit = index == place[q : q + 1]
        chosen[:, 128 * q : 128 * (q + 1)] = jnp.where(hit, 1.0, 0.0).astype(jnp.bfloat16)

    for index, (dr, dc) in enumerate(DIRECTIONS):
        @pl.when(there(-dr, -dc))
        def _(index=index):
            message(index).wait_recv()

    own_c, own_h = field[pl.ds(packed, GROUP)], halo[pl.ds(packed, GROUP)]
    lower = in_slot < 3
    faces = [
        (jnp.where(lower, side[:GROUP], own_c), jnp.where(lower, corner[:GROUP], own_h)),
        (jnp.where(lower, own_c, side[GROUP:]), jnp.where(lower, own_h, corner[GROUP:])),
    ]
    in_outer = jnp.where(row < 4, jnp.where(r < rows - 1, 1.0, 0.0), jnp.where(r > 0, 1.0, 0.0))
    in_left = jnp.where(lower, jnp.where(c > 0, 1.0, 0.0), 1.0)
    in_right = jnp.where(lower, 1.0, jnp.where(c < cols - 1, 1.0, 0.0))

    def joined(left, right):
        return jnp.where(in_slot == 7, roll_lanes(right, -4), roll_lanes(left, -2))

    def around_lanes(x, join, k):
        moved = roll_lanes(join, -SLOT * k)
        return jnp.where(east_end, moved, roll_lanes(x, -1)), jnp.where(west_end, moved, roll_lanes(x, 1))

    def replicate(x):
        x = jnp.where(slot == slots, x, 0.0)
        for step in (8, 16, 32, 64):
            x = x + roll_lanes(x, step)
        return x

    def weights(dc_, uc, vc, dh, uh, vh, lanes_c, lanes_h, mask_c, mask_h):
        dnc, dsc, dnh, dsh = around_rows(dc_, dh, first, last)
        vnc, vsc, vnh, vsh = around_rows(vc, vh, first, last)
        (dec, dwc), (uec, uwc) = lanes_c
        (deh, dwh), (ueh, uwh) = lanes_h
        wc = coefficients(dc_, uc, vc, dec, dwc, dnc, dsc, uec, uwc, vnc, vsc)
        wh = coefficients(dh, uh, vh, deh, dwh, dnh, dsh, ueh, uwh, vnh, vsh)
        if mask_c is not None:
            wc = tuple(w * mask_c for w in wc)
        return wc, tuple(w * mask_h for w in wh)

    face_w = []
    for (fc, fh), mask in zip(faces, (in_left, in_right)):
        dc_, uc, vc = (replicate(fc[i]) for i in range(3))
        dh, uh, vh = (replicate(fh[i]) for i in range(3))
        pair = lambda x: (roll_lanes(x, -1), roll_lanes(x, 1))
        face_w.append(weights(dc_, uc, vc, dh, uh, vh, (pair(dc_), pair(uc)), (pair(dh), pair(uh)), mask, mask * in_outer))
    join_c, join_h = joined(faces[0][0], faces[1][0]), joined(faces[0][1], faces[1][1])
    tile_c, tile_h = field[pl.ds(coef, 3)], halo[pl.ds(coef, 3)]
    lanes_c = tuple(around_lanes(tile_c[i], join_c[i], slots) for i in range(2))
    lanes_h = tuple(around_lanes(tile_h[i], join_h[i], slots) for i in range(2))
    wc, wh = weights(*(tile_c[i] for i in range(3)), *(tile_h[i] for i in range(3)), lanes_c, lanes_h, None, in_outer)

    for step in range(TRANSPORT_STEPS):
        final = step == TRANSPORT_STEPS - 1
        for k in range(slots):
            here = pl.ds(GROUP * k, GROUP)
            xc, xh = (field[here], halo[here]) if step == 0 else (next_c[here], next_h[here])
            nc, sc, nh, sh = around_rows(xc, xh, first, last)
            ec, wcc = around_lanes(xc, join_c, k)
            new = apply_step(wc, xc, ec, wcc, nc, sc)
            if final:
                adv[pl.ds(8 * GROUP * k, 8 * GROUP), :] = new.reshape(8 * GROUP, 128)
            else:
                eh, whh = around_lanes(xh, join_h, k)
                next_c[here] = new
                next_h[here] = apply_step(wh, xh, eh, whh, nh, sh)
        if not final:
            moved = []
            for (fc, fh), (fwc, fwh) in zip(faces, face_w):
                nc, sc, nh, sh = around_rows(fc, fh, first, last)
                moved.append((
                    apply_step(fwc, fc, roll_lanes(fc, -1), roll_lanes(fc, 1), nc, sc),
                    apply_step(fwh, fh, roll_lanes(fh, -1), roll_lanes(fh, 1), nh, sh),
                ))
            faces = moved
            join_c, join_h = joined(faces[0][0], faces[1][0]), joined(faces[0][1], faces[1][1])

    adv[pl.ds(8 * species, 8), :] = heat_v[...]
    adv[pl.ds(8 * (species + 1), 8 * (WIDTH - species - 1)), :] = jnp.zeros((8 * (WIDTH - species - 1), 128), jnp.float32)
    gathered = None
    for p in range(4):
        x = jnp.concatenate([adv[pl.ds(2 * p + j, WIDTH, stride=8), :] for j in range(2)], axis=1)
        terms = []
        for _ in range(3):
            terms.append(x.astype(jnp.bfloat16))
            x = x - terms[-1].astype(jnp.float32)
        part = lax.dot_general(
            chosen[:, 256 * p : 256 * (p + 1)], jnp.concatenate(terms, axis=0),
            (((1,), (1,)), ((), ())), preferred_element_type=jnp.float32,
        )
        gathered = part if gathered is None else gathered + part
    low = jnp.concatenate([gathered[:, 128:], jnp.zeros((capacity, WIDTH), jnp.float32)], axis=1)
    state = gathered[:, :128] + roll_lanes(gathered[:, :128], WIDTH) + low
    chunk = capacity // CHUNKS
    bases = [state[chunk * i : chunk * (i + 1)] for i in range(CHUNKS)]
    bias1, bias2, bias3 = b1_ref[...], b2_ref[...], b3_p[...]

    def substep(_, totals):
        hs = [(base + CHEM_STEP * total).astype(jnp.bfloat16) for base, total in zip(bases, totals)]
        hs = [jnp.dot(x, w1_p[...], preferred_element_type=jnp.float32) for x in hs]
        hs = [jnp.tanh(h + bias1).astype(jnp.bfloat16) for h in hs]
        hs = [jnp.dot(h, w2_p[...], preferred_element_type=jnp.float32) for h in hs]
        hs = [jnp.tanh(h + bias2).astype(jnp.bfloat16) for h in hs]
        hs = [jnp.dot(h, w3_p[...], preferred_element_type=jnp.float32) for h in hs]
        return tuple(total + (h + bias3) for total, h in zip(totals, hs))

    totals = tuple(jnp.zeros_like(b) for b in bases)
    totals = lax.fori_loop(0, SUBSTEPS, substep, totals, unroll=UNROLL)
    total = CHEM_STEP * jnp.transpose(jnp.concatenate(totals, axis=0))[:WIDTH]
    high = total.astype(jnp.bfloat16)
    low = (total - high.astype(jnp.float32)).astype(jnp.bfloat16)
    both = jnp.concatenate([high, low], axis=0)
    for p in range(4):
        part = jnp.dot(both, chosen[:, 256 * p : 256 * (p + 1)], preferred_element_type=jnp.float32)
        part = part[:WIDTH] + part[WIDTH:]
        for j in range(2):
            spread[pl.ds(WIDTH * (2 * p + j), WIDTH), :] = part[:, 128 * j : 128 * (j + 1)]
    for s in range(species):
        out_ref[s] = adv[pl.ds(8 * s, 8), :] + spread[pl.ds(s, 8, stride=WIDTH), :]

    for index, (dr, dc) in enumerate(DIRECTIONS):
        @pl.when(there(dr, dc))
        def _(index=index):
            message(index).wait_send()


def shards(rows, cols, mix, diff, speed, heat, active, w1, b1, w2, b2, w3, b3):
    species, height, width = mix.shape
    padded = pl.cdiv(species, GROUP) * GROUP
    fields = padded + 2 * GROUP
    hidden, features = w1.shape
    vm = pltpu.VMEM
    f32, bf16 = jnp.float32, jnp.bfloat16
    return pl.pallas_call(
        functools.partial(kernel, rows, cols, species),
        out_shape=jax.ShapeDtypeStruct(mix.shape, mix.dtype),
        in_specs=[pl.BlockSpec(memory_space=pltpu.HBM)] * 8 + [pl.BlockSpec(memory_space=vm)] * 3,
        out_specs=pl.BlockSpec(memory_space=vm),
        scratch_shapes=[
            vm((fields, height, width), f32),
            vm((fields, height, width), f32),
            vm((2 * GROUP, height, width), f32),
            vm((2 * GROUP, height, width), f32),
            vm((padded, height, width), f32),
            vm((padded, height, width), f32),
            vm((WIDTH * height, width), f32),
            vm((height, width), f32),
            vm((height, width), jnp.int32),
            vm((features, hidden), bf16),
            vm(w2.shape, bf16),
            vm(w3.shape, bf16),
            vm((128, hidden), bf16),
            vm((hidden, hidden), bf16),
            vm((128, hidden), bf16),
            vm((hidden, 128), bf16),
            vm((1, 128), f32),
            vm((3 * (height * width // 8), height * width), bf16),
            vm((WIDTH * height, width), f32),
            pltpu.SemaphoreType.DMA((8,)),
            pltpu.SemaphoreType.DMA((8,)),
            pltpu.SemaphoreType.DMA((8,)),
        ],
        compiler_params=pltpu.CompilerParams(collective_id=0, has_side_effects=True, vmem_limit_bytes=16 << 20),
    )(mix, diff, speed, heat, active, w1.T, w2, w3,
      b1[None], b2[None], b3[None])


def solution(mesh):
    tile = P(None, "row", "col")
    plane = P("row", "col")
    return jax.shard_map(
        functools.partial(shards, mesh.shape["row"], mesh.shape["col"]),
        mesh=mesh,
        in_specs=(tile, plane, tile, plane, plane, P(), P(), P(), P(), P(), P()),
        out_specs=tile,
        check_vma=False,
    )
```

```python
import functools

import jax
import jax.numpy as jnp
from jax import lax
from jax.experimental import pallas as pl
from jax.experimental.pallas import tpu as pltpu
from jax.sharding import PartitionSpec as P

SUBSTEPS = 8
TRANSPORT_STEPS = 3
CHEM_STEP = 0.0625
GROUP = 4
SLOT = 8
CHUNKS = 2
WIDTH = 64
UNROLL = 1
MESH_ID = pl.DeviceIdType.MESH
DIRECTIONS = tuple((dr, dc) for dr in (-1, 0, 1) for dc in (-1, 0, 1) if (dr, dc) != (0, 0))


def roll_lanes(x, shift):
    return pltpu.roll(x, shift % x.shape[-1], x.ndim - 1)


def roll_rows(x, shift):
    return pltpu.roll(x, shift % x.shape[-2], x.ndim - 2)


def around_rows(centre, outer, first, last):
    cu, hu = roll_rows(centre, -1), roll_rows(outer, -1)
    cd, hd = roll_rows(centre, 1), roll_rows(outer, 1)
    return (
        jnp.where(last, hu, cu),
        jnp.where(first, hd, cd),
        jnp.where(last, cu, hu),
        jnp.where(first, cd, hd),
    )


def coefficients(d, u, v, de, dw, dn, ds, ue, uw, vn, vs):
    de, dw, dn, ds = (0.5 * (d + x) for x in (de, dw, dn, ds))
    ue, uw, vn, vs = 0.5 * (u + ue), 0.5 * (u + uw), 0.5 * (v + vn), 0.5 * (v + vs)
    own = (
        1.0
        - (de + jnp.maximum(ue, 0.0))
        - (dw - jnp.minimum(uw, 0.0))
        - (dn + jnp.maximum(vn, 0.0))
        - (ds - jnp.minimum(vs, 0.0))
    )
    return (
        own,
        de - jnp.minimum(ue, 0.0),
        dw + jnp.maximum(uw, 0.0),
        dn - jnp.minimum(vn, 0.0),
        ds + jnp.maximum(vs, 0.0),
    )


def apply_step(w, own, east, west, north, south):
    return w[0] * own + w[1] * east + w[2] * west + w[3] * north + w[4] * south


def kernel(
    rows, cols, species,
    mix_hbm, diff_hbm, speed_hbm, heat_hbm, active_hbm, w1_hbm, w2_hbm, w3_hbm,
    b1_hbm, b2_hbm, b3_hbm,
    out_ref,
    b1_ref, b2_ref, b3_ref,
    field, halo, side, corner, next_c, next_h, adv, heat_v, active_v, w1_v, w2_v, w3_v, w1_p, w2_p, w3_s, w3_p, b3_p, chosen, spread,
    local_sem, send_sem, recv_sem,
):
    r, c = lax.axis_index("row"), lax.axis_index("col")
    padded = pl.cdiv(species, GROUP) * GROUP
    slots = padded // GROUP
    coef = padded
    packed = padded + GROUP

    loads = [
        pltpu.make_async_copy(mix_hbm, field.at[pl.ds(0, species)], local_sem.at[0]),
        pltpu.make_async_copy(diff_hbm, field.at[coef], local_sem.at[1]),
        pltpu.make_async_copy(speed_hbm, field.at[pl.ds(coef + 1, 2)], local_sem.at[2]),
        pltpu.make_async_copy(heat_hbm, heat_v, local_sem.at[3]),
        pltpu.make_async_copy(active_hbm, active_v, local_sem.at[4]),
        pltpu.make_async_copy(w1_hbm, w1_v, local_sem.at[5]),
        pltpu.make_async_copy(w2_hbm, w2_v, local_sem.at[6]),
        pltpu.make_async_copy(w3_hbm, w3_v, local_sem.at[7]),
        pltpu.make_async_copy(b1_hbm, b1_ref, local_sem.at[8]),
        pltpu.make_async_copy(b2_hbm, b2_ref, local_sem.at[9]),
        pltpu.make_async_copy(b3_hbm, b3_ref, local_sem.at[10]),
    ]
    for load in loads:
        load.start()
    halo[...] = jnp.zeros_like(halo)
    side[...] = jnp.zeros_like(side)
    corner[...] = jnp.zeros_like(corner)

    def there(dr, dc):
        ok = jnp.bool_(True)
        if dr:
            ok = jnp.logical_and(ok, r + dr < rows if dr > 0 else r + dr >= 0)
        if dc:
            ok = jnp.logical_and(ok, c + dc < cols if dc > 0 else c + dc >= 0)
        return ok

    barrier = pltpu.get_barrier_semaphore()
    for dr, dc in DIRECTIONS:
        @pl.when(there(dr, dc))
        def _(dr=dr, dc=dc):
            pl.semaphore_signal(barrier, inc=1, device_id=(r + dr, c + dc), device_id_type=MESH_ID)

    for s in [*range(species, padded), coef + 3]:
        field[s] = jnp.zeros(field.shape[1:], jnp.float32)
    lane = lax.broadcasted_iota(jnp.int32, (8, 128), 1)
    row = lax.broadcasted_iota(jnp.int32, (8, 128), 0)
    first, last = row == 0, row == 7
    west_end, east_end = lane == 0, lane == 127
    in_slot = lane % SLOT
    slot = lane // SLOT
    for load in loads[:3]:
        load.wait()
    pack = jnp.zeros((GROUP, 8, 128), jnp.float32)
    for k in range(slots + 1):
        pack = jnp.where(slot == k, roll_lanes(field[pl.ds(GROUP * k, GROUP)], SLOT * k + 3), pack)
    field[pl.ds(packed, GROUP)] = pack

    one = lambda ok: jnp.where(ok, 1, 0)
    row_sides, col_sides = one(r > 0) + one(r < rows - 1), one(c > 0) + one(c < cols - 1)
    pl.semaphore_wait(barrier, (1 + row_sides) * (1 + col_sides) - 1)

    def message(index):
        dr, dc = DIRECTIONS[index]
        strip = {1: pl.ds(5, 3), -1: pl.ds(0, 3), 0: pl.ds(0, 8)}[dr]
        if dc == 0:
            src, dst = field.at[:, strip, :], halo.at[:, strip, :]
        else:
            target = side if dr == 0 else corner
            src = field.at[pl.ds(packed, GROUP), strip, :]
            dst = target.at[pl.ds(0 if dc > 0 else GROUP, GROUP), strip, :]
        return pltpu.make_async_remote_copy(
            src_ref=src, dst_ref=dst, send_sem=send_sem.at[index], recv_sem=recv_sem.at[index],
            device_id=(r + dr, c + dc), device_id_type=MESH_ID,
        )

    for index, (dr, dc) in enumerate(DIRECTIONS):
        @pl.when(there(dr, dc))
        def _(index=index):
            message(index).start()

    for load in loads[3:]:
        load.wait()
    w1_p[...] = jnp.zeros_like(w1_p)
    w1_p[pl.ds(0, species + 1), :] = w1_v[...]
    w2_p[...] = jnp.transpose(w2_v[...].astype(jnp.float32)).astype(jnp.bfloat16)
    w3_s[...] = jnp.zeros_like(w3_s)
    w3_s[pl.ds(0, species), :] = w3_v[...]
    w3_p[...] = jnp.transpose(w3_s[...].astype(jnp.float32)).astype(jnp.bfloat16)
    b3_p[...] = jnp.zeros_like(b3_p)
    b3_p[:, pl.ds(0, species)] = b3_ref[...]

    capacity = chosen.shape[0]
    flags = jnp.where(active_v[...] == 1, 1.0, 0.0)
    upto = lax.broadcasted_iota(jnp.int32, (128, 128), 0) <= lax.broadcasted_iota(jnp.int32, (128, 128), 1)
    upto = jnp.where(upto, 1.0, 0.0).astype(jnp.bfloat16)
    within = jnp.dot(flags.astype(jnp.bfloat16), upto, preferred_element_type=jnp.float32)
    offset = jnp.dot(flags.astype(jnp.bfloat16), jnp.ones((128, 128), jnp.bfloat16), preferred_element_type=jnp.float32)
    offset = jnp.where(row >= 1, roll_rows(offset, 1), 0.0)
    for shift in (1, 2, 4):
        offset = offset + jnp.where(row >= shift, roll_rows(offset, shift), 0.0)
    place = jnp.where(flags > 0.0, within + offset - 1.0, -1.0)
    index = lax.broadcasted_iota(jnp.int32, (capacity, 128), 0).astype(jnp.float32)
    for q in range(8):
        hit = index == place[q : q + 1]
        chosen[:, 128 * q : 128 * (q + 1)] = jnp.where(hit, 1.0, 0.0).astype(jnp.bfloat16)

    for index, (dr, dc) in enumerate(DIRECTIONS):
        @pl.when(there(-dr, -dc))
        def _(index=index):
            message(index).wait_recv()

    own_c, own_h = field[pl.ds(packed, GROUP)], halo[pl.ds(packed, GROUP)]
    lower = in_slot < 3
    faces = [
        (jnp.where(lower, side[:GROUP], own_c), jnp.where(lower, corner[:GROUP], own_h)),
        (jnp.where(lower, own_c, side[GROUP:]), jnp.where(lower, own_h, corner[GROUP:])),
    ]
    in_outer = jnp.where(row < 4, jnp.where(r < rows - 1, 1.0, 0.0), jnp.where(r > 0, 1.0, 0.0))
    in_left = jnp.where(lower, jnp.where(c > 0, 1.0, 0.0), 1.0)
    in_right = jnp.where(lower, 1.0, jnp.where(c < cols - 1, 1.0, 0.0))

    def joined(left, right):
        return jnp.where(in_slot == 7, roll_lanes(right, -4), roll_lanes(left, -2))

    def around_lanes(x, join, k):
        moved = roll_lanes(join, -SLOT * k)
        return jnp.where(east_end, moved, roll_lanes(x, -1)), jnp.where(west_end, moved, roll_lanes(x, 1))

    def replicate(x):
        x = jnp.where(slot == slots, x, 0.0)
        for step in (8, 16, 32, 64):
            x = x + roll_lanes(x, step)
        return x

    def weights(dc_, uc, vc, dh, uh, vh, lanes_c, lanes_h, mask_c, mask_h):
        dnc, dsc, dnh, dsh = around_rows(dc_, dh, first, last)
        vnc, vsc, vnh, vsh = around_rows(vc, vh, first, last)
        (dec, dwc), (uec, uwc) = lanes_c
        (deh, dwh), (ueh, uwh) = lanes_h
        wc = coefficients(dc_, uc, vc, dec, dwc, dnc, dsc, uec, uwc, vnc, vsc)
        wh = coefficients(dh, uh, vh, deh, dwh, dnh, dsh, ueh, uwh, vnh, vsh)
        if mask_c is not None:
            wc = tuple(w * mask_c for w in wc)
        return wc, tuple(w * mask_h for w in wh)

    face_w = []
    for (fc, fh), mask in zip(faces, (in_left, in_right)):
        dc_, uc, vc = (replicate(fc[i]) for i in range(3))
        dh, uh, vh = (replicate(fh[i]) for i in range(3))
        pair = lambda x: (roll_lanes(x, -1), roll_lanes(x, 1))
        face_w.append(weights(dc_, uc, vc, dh, uh, vh, (pair(dc_), pair(uc)), (pair(dh), pair(uh)), mask, mask * in_outer))
    join_c, join_h = joined(faces[0][0], faces[1][0]), joined(faces[0][1], faces[1][1])
    tile_c, tile_h = field[pl.ds(coef, 3)], halo[pl.ds(coef, 3)]
    lanes_c = tuple(around_lanes(tile_c[i], join_c[i], slots) for i in range(2))
    lanes_h = tuple(around_lanes(tile_h[i], join_h[i], slots) for i in range(2))
    wc, wh = weights(*(tile_c[i] for i in range(3)), *(tile_h[i] for i in range(3)), lanes_c, lanes_h, None, in_outer)

    for step in range(TRANSPORT_STEPS):
        final = step == TRANSPORT_STEPS - 1
        for k in range(slots):
            here = pl.ds(GROUP * k, GROUP)
            xc, xh = (field[here], halo[here]) if step == 0 else (next_c[here], next_h[here])
            nc, sc, nh, sh = around_rows(xc, xh, first, last)
            ec, wcc = around_lanes(xc, join_c, k)
            new = apply_step(wc, xc, ec, wcc, nc, sc)
            if final:
                adv[pl.ds(8 * GROUP * k, 8 * GROUP), :] = new.reshape(8 * GROUP, 128)
            else:
                eh, whh = around_lanes(xh, join_h, k)
                next_c[here] = new
                next_h[here] = apply_step(wh, xh, eh, whh, nh, sh)
        if not final:
            moved = []
            for (fc, fh), (fwc, fwh) in zip(faces, face_w):
                nc, sc, nh, sh = around_rows(fc, fh, first, last)
                moved.append((
                    apply_step(fwc, fc, roll_lanes(fc, -1), roll_lanes(fc, 1), nc, sc),
                    apply_step(fwh, fh, roll_lanes(fh, -1), roll_lanes(fh, 1), nh, sh),
                ))
            faces = moved
            join_c, join_h = joined(faces[0][0], faces[1][0]), joined(faces[0][1], faces[1][1])

    adv[pl.ds(8 * species, 8), :] = heat_v[...]
    adv[pl.ds(8 * (species + 1), 8 * (WIDTH - species - 1)), :] = jnp.zeros((8 * (WIDTH - species - 1), 128), jnp.float32)
    gathered = None
    for p in range(4):
        x = jnp.concatenate([adv[pl.ds(2 * p + j, WIDTH, stride=8), :] for j in range(2)], axis=1)
        terms = []
        for _ in range(3):
            terms.append(x.astype(jnp.bfloat16))
            x = x - terms[-1].astype(jnp.float32)
        part = lax.dot_general(
            chosen[:, 256 * p : 256 * (p + 1)], jnp.concatenate(terms, axis=0),
            (((1,), (1,)), ((), ())), preferred_element_type=jnp.float32,
        )
        gathered = part if gathered is None else gathered + part
    low = jnp.concatenate([gathered[:, 128:], jnp.zeros((capacity, WIDTH), jnp.float32)], axis=1)
    state = gathered[:, :128] + roll_lanes(gathered[:, :128], WIDTH) + low
    chunk = capacity // CHUNKS
    bases = [state[chunk * i : chunk * (i + 1)] for i in range(CHUNKS)]
    bias1, bias2, bias3 = b1_ref[...], b2_ref[...], b3_p[...]

    def substep(_, totals):
        hs = [(base + CHEM_STEP * total).astype(jnp.bfloat16) for base, total in zip(bases, totals)]
        hs = [jnp.dot(x, w1_p[...], preferred_element_type=jnp.float32) for x in hs]
        hs = [jnp.tanh(h + bias1).astype(jnp.bfloat16) for h in hs]
        hs = [jnp.dot(h, w2_p[...], preferred_element_type=jnp.float32) for h in hs]
        hs = [jnp.tanh(h + bias2).astype(jnp.bfloat16) for h in hs]
        hs = [jnp.dot(h, w3_p[...], preferred_element_type=jnp.float32) for h in hs]
        return tuple(total + (h + bias3) for total, h in zip(totals, hs))

    totals = tuple(jnp.zeros_like(b) for b in bases)
    totals = lax.fori_loop(0, SUBSTEPS, substep, totals, unroll=UNROLL)
    total = CHEM_STEP * jnp.transpose(jnp.concatenate(totals, axis=0))[:WIDTH]
    high = total.astype(jnp.bfloat16)
    low = (total - high.astype(jnp.float32)).astype(jnp.bfloat16)
    both = jnp.concatenate([high, low], axis=0)
    for p in range(4):
        part = jnp.dot(both, chosen[:, 256 * p : 256 * (p + 1)], preferred_element_type=jnp.float32)
        part = part[:WIDTH] + part[WIDTH:]
        for j in range(2):
            spread[pl.ds(WIDTH * (2 * p + j), WIDTH), :] = part[:, 128 * j : 128 * (j + 1)]
    for s in range(species):
        out_ref[s] = adv[pl.ds(8 * s, 8), :] + spread[pl.ds(s, 8, stride=WIDTH), :]

    for index, (dr, dc) in enumerate(DIRECTIONS):
        @pl.when(there(dr, dc))
        def _(index=index):
            message(index).wait_send()


def shards(rows, cols, mix, diff, speed, heat, active, w1, b1, w2, b2, w3, b3):
    species, height, width = mix.shape
    padded = pl.cdiv(species, GROUP) * GROUP
    fields = padded + 2 * GROUP
    hidden, features = w1.shape
    vm = pltpu.VMEM
    f32, bf16 = jnp.float32, jnp.bfloat16
    held = lambda x: pltpu.with_memory_space_constraint(x, pltpu.HBM)
    return pl.pallas_call(
        functools.partial(kernel, rows, cols, species),
        out_shape=jax.ShapeDtypeStruct(mix.shape, mix.dtype),
        in_specs=[pl.BlockSpec(memory_space=pltpu.HBM)] * 11,
        out_specs=pl.BlockSpec(memory_space=vm),
        scratch_shapes=[
            vm((1, hidden), f32),
            vm((1, hidden), f32),
            vm((1, species), f32),
            vm((fields, height, width), f32),
            vm((fields, height, width), f32),
            vm((2 * GROUP, height, width), f32),
            vm((2 * GROUP, height, width), f32),
            vm((padded, height, width), f32),
            vm((padded, height, width), f32),
            vm((WIDTH * height, width), f32),
            vm((height, width), f32),
            vm((height, width), jnp.int32),
            vm((features, hidden), bf16),
            vm(w2.shape, bf16),
            vm(w3.shape, bf16),
            vm((128, hidden), bf16),
            vm((hidden, hidden), bf16),
            vm((128, hidden), bf16),
            vm((hidden, 128), bf16),
            vm((1, 128), f32),
            vm((3 * (height * width // 8), height * width), bf16),
            vm((WIDTH * height, width), f32),
            pltpu.SemaphoreType.DMA((11,)),
            pltpu.SemaphoreType.DMA((8,)),
            pltpu.SemaphoreType.DMA((8,)),
        ],
        compiler_params=pltpu.CompilerParams(collective_id=0, has_side_effects=True, vmem_limit_bytes=16 << 20),
    )(*(held(x) for x in (mix, diff, speed, heat, active, w1.T, w2, w3, b1[None], b2[None], b3[None])))


def solution(mesh):
    tile = P(None, "row", "col")
    plane = P("row", "col")
    return jax.shard_map(
        functools.partial(shards, mesh.shape["row"], mesh.shape["col"]),
        mesh=mesh,
        in_specs=(tile, plane, tile, plane, plane, P(), P(), P(), P(), P(), P()),
        out_specs=tile,
        check_vma=False,
    )
```

```python
import functools

import jax
import jax.numpy as jnp
from jax import lax
from jax.experimental import pallas as pl
from jax.experimental.pallas import tpu as pltpu
from jax.sharding import PartitionSpec as P

SUBSTEPS = 8
TRANSPORT_STEPS = 3
CHEM_STEP = 0.0625
GROUP = 4
SLOT = 8
CHUNKS = 2
WIDTH = 64
UNROLL = 1
PIECE = 4
MESH_ID = pl.DeviceIdType.MESH
DIRECTIONS = tuple((dr, dc) for dr in (-1, 0, 1) for dc in (-1, 0, 1) if (dr, dc) != (0, 0))


def roll_lanes(x, shift):
    return pltpu.roll(x, shift % x.shape[-1], x.ndim - 1)


def roll_rows(x, shift):
    return pltpu.roll(x, shift % x.shape[-2], x.ndim - 2)


def around_rows(centre, outer, first, last):
    cu, hu = roll_rows(centre, -1), roll_rows(outer, -1)
    cd, hd = roll_rows(centre, 1), roll_rows(outer, 1)
    return (
        jnp.where(last, hu, cu),
        jnp.where(first, hd, cd),
        jnp.where(last, cu, hu),
        jnp.where(first, cd, hd),
    )


def coefficients(d, u, v, de, dw, dn, ds, ue, uw, vn, vs):
    de, dw, dn, ds = (0.5 * (d + x) for x in (de, dw, dn, ds))
    ue, uw, vn, vs = 0.5 * (u + ue), 0.5 * (u + uw), 0.5 * (v + vn), 0.5 * (v + vs)
    own = (
        1.0
        - (de + jnp.maximum(ue, 0.0))
        - (dw - jnp.minimum(uw, 0.0))
        - (dn + jnp.maximum(vn, 0.0))
        - (ds - jnp.minimum(vs, 0.0))
    )
    return (
        own,
        de - jnp.minimum(ue, 0.0),
        dw + jnp.maximum(uw, 0.0),
        dn - jnp.minimum(vn, 0.0),
        ds + jnp.maximum(vs, 0.0),
    )


def apply_step(w, own, east, west, north, south):
    return w[0] * own + w[1] * east + w[2] * west + w[3] * north + w[4] * south


def kernel(
    rows, cols, species,
    mix_hbm, diff_hbm, speed_hbm, heat_hbm, active_hbm, w1_hbm, w2_hbm, w3_hbm,
    b1_hbm, b2_hbm, b3_hbm,
    out_ref,
    b1_ref, b2_ref, b3_ref,
    field, halo, side, corner, weight, joins, adv, heat_v, active_v, w1_v, w2_v, w3_v, w1_p, w2_p, w3_s, w3_p, b3_p, chosen, spread,
    local_sem, send_sem, recv_sem,
):
    r, c = lax.axis_index("row"), lax.axis_index("col")
    padded = pl.cdiv(species, GROUP) * GROUP
    slots = padded // GROUP
    coef = padded
    packed = padded + GROUP

    loads = [
        pltpu.make_async_copy(mix_hbm, field.at[pl.ds(0, species)], local_sem.at[0]),
        pltpu.make_async_copy(diff_hbm, field.at[coef], local_sem.at[1]),
        pltpu.make_async_copy(speed_hbm, field.at[pl.ds(coef + 1, 2)], local_sem.at[2]),
        pltpu.make_async_copy(heat_hbm, heat_v, local_sem.at[3]),
        pltpu.make_async_copy(active_hbm, active_v, local_sem.at[4]),
        pltpu.make_async_copy(w1_hbm, w1_v, local_sem.at[5]),
        pltpu.make_async_copy(w2_hbm, w2_v, local_sem.at[6]),
        pltpu.make_async_copy(w3_hbm, w3_v, local_sem.at[7]),
        pltpu.make_async_copy(b1_hbm, b1_ref, local_sem.at[8]),
        pltpu.make_async_copy(b2_hbm, b2_ref, local_sem.at[9]),
        pltpu.make_async_copy(b3_hbm, b3_ref, local_sem.at[10]),
    ]
    for load in loads:
        load.start()
    halo[...] = jnp.zeros_like(halo)
    side[...] = jnp.zeros_like(side)
    corner[...] = jnp.zeros_like(corner)

    def there(dr, dc):
        ok = jnp.bool_(True)
        if dr:
            ok = jnp.logical_and(ok, r + dr < rows if dr > 0 else r + dr >= 0)
        if dc:
            ok = jnp.logical_and(ok, c + dc < cols if dc > 0 else c + dc >= 0)
        return ok

    barrier = pltpu.get_barrier_semaphore()
    for dr, dc in DIRECTIONS:
        @pl.when(there(dr, dc))
        def _(dr=dr, dc=dc):
            pl.semaphore_signal(barrier, inc=1, device_id=(r + dr, c + dc), device_id_type=MESH_ID)

    for s in [*range(species, padded), coef + 3]:
        field[s] = jnp.zeros(field.shape[1:], jnp.float32)
    lane = lax.broadcasted_iota(jnp.int32, (8, 128), 1)
    row = lax.broadcasted_iota(jnp.int32, (8, 128), 0)
    first, last = row == 0, row == 7
    west_end, east_end = lane == 0, lane == 127
    in_slot = lane % SLOT
    slot = lane // SLOT
    for load in loads[:3]:
        load.wait()
    pack = jnp.zeros((GROUP, 8, 128), jnp.float32)
    for k in range(slots + 1):
        pack = jnp.where(slot == k, roll_lanes(field[pl.ds(GROUP * k, GROUP)], SLOT * k + 3), pack)
    field[pl.ds(packed, GROUP)] = pack

    one = lambda ok: jnp.where(ok, 1, 0)
    row_sides, col_sides = one(r > 0) + one(r < rows - 1), one(c > 0) + one(c < cols - 1)
    pl.semaphore_wait(barrier, (1 + row_sides) * (1 + col_sides) - 1)

    pieces = [(packed - GROUP, 2 * GROUP)] + [
        (GROUP * k, GROUP * min(PIECE, slots - k)) for k in range(0, slots, PIECE)
    ]

    def message(index, piece=0):
        dr, dc = DIRECTIONS[index]
        strip = {1: pl.ds(5, 3), -1: pl.ds(0, 3), 0: pl.ds(0, 8)}[dr]
        if dc == 0:
            some = pl.ds(*pieces[piece])
            src, dst = field.at[some, strip, :], halo.at[some, strip, :]
        else:
            target = side if dr == 0 else corner
            src = field.at[pl.ds(packed, GROUP), strip, :]
            dst = target.at[pl.ds(0 if dc > 0 else GROUP, GROUP), strip, :]
        return pltpu.make_async_remote_copy(
            src_ref=src, dst_ref=dst, send_sem=send_sem.at[index, piece], recv_sem=recv_sem.at[index, piece],
            device_id=(r + dr, c + dc), device_id_type=MESH_ID,
        )

    def for_each(action, numbers, sign):
        for number in numbers:
            for index, (dr, dc) in enumerate(DIRECTIONS):
                if number and dc:
                    continue

                @pl.when(there(sign * dr, sign * dc))
                def _(index=index, number=number):
                    action(message(index, number))

    def arrive(begin):
        for_each(lambda m: m.wait_recv(), [1 + begin // PIECE], -1)

    everything = range(len(pieces))
    for_each(lambda m: m.start(), everything, 1)

    for load in loads[3:]:
        load.wait()
    w1_p[...] = jnp.zeros_like(w1_p)
    w1_p[pl.ds(0, species + 1), :] = w1_v[...]
    w2_p[...] = jnp.transpose(w2_v[...].astype(jnp.float32)).astype(jnp.bfloat16)
    w3_s[...] = jnp.zeros_like(w3_s)
    w3_s[pl.ds(0, species), :] = w3_v[...]
    w3_p[...] = jnp.transpose(w3_s[...].astype(jnp.float32)).astype(jnp.bfloat16)
    b3_p[...] = jnp.zeros_like(b3_p)
    b3_p[:, pl.ds(0, species)] = b3_ref[...]

    capacity = chosen.shape[0]
    flags = jnp.where(active_v[...] == 1, 1.0, 0.0)
    upto = lax.broadcasted_iota(jnp.int32, (128, 128), 0) <= lax.broadcasted_iota(jnp.int32, (128, 128), 1)
    upto = jnp.where(upto, 1.0, 0.0).astype(jnp.bfloat16)
    within = jnp.dot(flags.astype(jnp.bfloat16), upto, preferred_element_type=jnp.float32)
    offset = jnp.dot(flags.astype(jnp.bfloat16), jnp.ones((128, 128), jnp.bfloat16), preferred_element_type=jnp.float32)
    offset = jnp.where(row >= 1, roll_rows(offset, 1), 0.0)
    for shift in (1, 2, 4):
        offset = offset + jnp.where(row >= shift, roll_rows(offset, shift), 0.0)
    place = jnp.where(flags > 0.0, within + offset - 1.0, -1.0)
    index = lax.broadcasted_iota(jnp.int32, (capacity, 128), 0).astype(jnp.float32)
    for q in range(8):
        hit = index == place[q : q + 1]
        chosen[:, 128 * q : 128 * (q + 1)] = jnp.where(hit, 1.0, 0.0).astype(jnp.bfloat16)

    for_each(lambda m: m.wait_recv(), [0], -1)

    own_c, own_h = field[pl.ds(packed, GROUP)], halo[pl.ds(packed, GROUP)]
    lower = in_slot < 3
    faces = [
        (jnp.where(lower, side[:GROUP], own_c), jnp.where(lower, corner[:GROUP], own_h)),
        (jnp.where(lower, own_c, side[GROUP:]), jnp.where(lower, own_h, corner[GROUP:])),
    ]
    in_outer = jnp.where(row < 4, jnp.where(r < rows - 1, 1.0, 0.0), jnp.where(r > 0, 1.0, 0.0))
    in_left = jnp.where(lower, jnp.where(c > 0, 1.0, 0.0), 1.0)
    in_right = jnp.where(lower, 1.0, jnp.where(c < cols - 1, 1.0, 0.0))

    def joined(left, right):
        return jnp.where(in_slot == 7, roll_lanes(right, -4), roll_lanes(left, -2))

    def around_lanes(x, join, k):
        moved = roll_lanes(join, -SLOT * k)
        return jnp.where(east_end, moved, roll_lanes(x, -1)), jnp.where(west_end, moved, roll_lanes(x, 1))

    def replicate(x):
        x = jnp.where(slot == slots, x, 0.0)
        for step in (8, 16, 32, 64):
            x = x + roll_lanes(x, step)
        return x

    def weights(dc_, uc, vc, dh, uh, vh, lanes_c, lanes_h, mask_c, mask_h):
        dnc, dsc, dnh, dsh = around_rows(dc_, dh, first, last)
        vnc, vsc, vnh, vsh = around_rows(vc, vh, first, last)
        (dec, dwc), (uec, uwc) = lanes_c
        (deh, dwh), (ueh, uwh) = lanes_h
        wc = coefficients(dc_, uc, vc, dec, dwc, dnc, dsc, uec, uwc, vnc, vsc)
        wh = coefficients(dh, uh, vh, deh, dwh, dnh, dsh, ueh, uwh, vnh, vsh)
        if mask_c is not None:
            wc = tuple(w * mask_c for w in wc)
        return wc, tuple(w * mask_h for w in wh)

    face_w = []
    for (fc, fh), mask in zip(faces, (in_left, in_right)):
        dc_, uc, vc = (replicate(fc[i]) for i in range(3))
        dh, uh, vh = (replicate(fh[i]) for i in range(3))
        pair = lambda x: (roll_lanes(x, -1), roll_lanes(x, 1))
        face_w.append(weights(dc_, uc, vc, dh, uh, vh, (pair(dc_), pair(uc)), (pair(dh), pair(uh)), mask, mask * in_outer))
    join_c, join_h = joined(faces[0][0], faces[1][0]), joined(faces[0][1], faces[1][1])
    tile_c, tile_h = field[pl.ds(coef, 3)], halo[pl.ds(coef, 3)]
    lanes_c = tuple(around_lanes(tile_c[i], join_c[i], slots) for i in range(2))
    lanes_h = tuple(around_lanes(tile_h[i], join_h[i], slots) for i in range(2))
    wc, wh = weights(*(tile_c[i] for i in range(3)), *(tile_h[i] for i in range(3)), lanes_c, lanes_h, None, in_outer)

    for i in range(5):
        weight[i] = wc[i]
        weight[5 + i] = wh[i]
    for step in range(TRANSPORT_STEPS):
        joins[2 * step] = joined(faces[0][0], faces[1][0])
        joins[2 * step + 1] = joined(faces[0][1], faces[1][1])
        if step < TRANSPORT_STEPS - 1:
            moved = []
            for (fc, fh), (fwc, fwh) in zip(faces, face_w):
                nc, sc, nh, sh = around_rows(fc, fh, first, last)
                moved.append((
                    apply_step(fwc, fc, roll_lanes(fc, -1), roll_lanes(fc, 1), nc, sc),
                    apply_step(fwh, fh, roll_lanes(fh, -1), roll_lanes(fh, 1), nh, sh),
                ))
            faces = moved

    def advance_group(k):
        here = pl.ds(GROUP * k, GROUP)
        xc, xh = field[here], halo[here]
        for step in range(TRANSPORT_STEPS):
            nc, sc, nh, sh = around_rows(xc, xh, first, last)
            ec, wcc = around_lanes(xc, joins[2 * step], k)
            new = apply_step([weight[i] for i in range(5)], xc, ec, wcc, nc, sc)
            if step < TRANSPORT_STEPS - 1:
                eh, whh = around_lanes(xh, joins[2 * step + 1], k)
                xh = apply_step([weight[5 + i] for i in range(5)], xh, eh, whh, nh, sh)
            xc = new
        adv[pl.ds(8 * GROUP * k, 8 * GROUP), :] = xc.reshape(8 * GROUP, 128)

    for begin in range(0, slots, PIECE):
        arrive(begin)
        for k in range(begin, min(begin + PIECE, slots)):
            advance_group(k)

    adv[pl.ds(8 * species, 8), :] = heat_v[...]
    adv[pl.ds(8 * (species + 1), 8 * (WIDTH - species - 1)), :] = jnp.zeros((8 * (WIDTH - species - 1), 128), jnp.float32)
    gathered = None
    for p in range(4):
        x = jnp.concatenate([adv[pl.ds(2 * p + j, WIDTH, stride=8), :] for j in range(2)], axis=1)
        terms = []
        for _ in range(3):
            terms.append(x.astype(jnp.bfloat16))
            x = x - terms[-1].astype(jnp.float32)
        part = lax.dot_general(
            chosen[:, 256 * p : 256 * (p + 1)], jnp.concatenate(terms, axis=0),
            (((1,), (1,)), ((), ())), preferred_element_type=jnp.float32,
        )
        gathered = part if gathered is None else gathered + part
    low = jnp.concatenate([gathered[:, 128:], jnp.zeros((capacity, WIDTH), jnp.float32)], axis=1)
    state = gathered[:, :128] + roll_lanes(gathered[:, :128], WIDTH) + low
    chunk = capacity // CHUNKS
    bases = [state[chunk * i : chunk * (i + 1)] for i in range(CHUNKS)]
    bias1, bias2, bias3 = b1_ref[...], b2_ref[...], b3_p[...]

    def substep(_, totals):
        hs = [(base + CHEM_STEP * total).astype(jnp.bfloat16) for base, total in zip(bases, totals)]
        hs = [jnp.dot(x, w1_p[...], preferred_element_type=jnp.float32) for x in hs]
        hs = [jnp.tanh(h + bias1).astype(jnp.bfloat16) for h in hs]
        hs = [jnp.dot(h, w2_p[...], preferred_element_type=jnp.float32) for h in hs]
        hs = [jnp.tanh(h + bias2).astype(jnp.bfloat16) for h in hs]
        hs = [jnp.dot(h, w3_p[...], preferred_element_type=jnp.float32) for h in hs]
        return tuple(total + (h + bias3) for total, h in zip(totals, hs))

    totals = tuple(jnp.zeros_like(b) for b in bases)
    totals = lax.fori_loop(0, SUBSTEPS, substep, totals, unroll=UNROLL)
    total = CHEM_STEP * jnp.transpose(jnp.concatenate(totals, axis=0))[:WIDTH]
    high = total.astype(jnp.bfloat16)
    low = (total - high.astype(jnp.float32)).astype(jnp.bfloat16)
    both = jnp.concatenate([high, low], axis=0)
    for p in range(4):
        part = jnp.dot(both, chosen[:, 256 * p : 256 * (p + 1)], preferred_element_type=jnp.float32)
        part = part[:WIDTH] + part[WIDTH:]
        for j in range(2):
            spread[pl.ds(WIDTH * (2 * p + j), WIDTH), :] = part[:, 128 * j : 128 * (j + 1)]
    for s in range(species):
        out_ref[s] = adv[pl.ds(8 * s, 8), :] + spread[pl.ds(s, 8, stride=WIDTH), :]

    for_each(lambda m: m.wait_send(), everything, 1)


def shards(rows, cols, mix, diff, speed, heat, active, w1, b1, w2, b2, w3, b3):
    species, height, width = mix.shape
    padded = pl.cdiv(species, GROUP) * GROUP
    fields = padded + 2 * GROUP
    hidden, features = w1.shape
    parts = 1 + pl.cdiv(padded // GROUP, PIECE)
    vm = pltpu.VMEM
    f32, bf16 = jnp.float32, jnp.bfloat16
    held = lambda x: pltpu.with_memory_space_constraint(x, pltpu.HBM)
    return pl.pallas_call(
        functools.partial(kernel, rows, cols, species),
        out_shape=jax.ShapeDtypeStruct(mix.shape, mix.dtype),
        in_specs=[pl.BlockSpec(memory_space=pltpu.HBM)] * 11,
        out_specs=pl.BlockSpec(memory_space=vm),
        scratch_shapes=[
            vm((1, hidden), f32),
            vm((1, hidden), f32),
            vm((1, species), f32),
            vm((fields, height, width), f32),
            vm((fields, height, width), f32),
            vm((2 * GROUP, height, width), f32),
            vm((2 * GROUP, height, width), f32),
            vm((10, height, width), f32),
            vm((2 * TRANSPORT_STEPS, GROUP, height, width), f32),
            vm((WIDTH * height, width), f32),
            vm((height, width), f32),
            vm((height, width), jnp.int32),
            vm((features, hidden), bf16),
            vm(w2.shape, bf16),
            vm(w3.shape, bf16),
            vm((128, hidden), bf16),
            vm((hidden, hidden), bf16),
            vm((128, hidden), bf16),
            vm((hidden, 128), bf16),
            vm((1, 128), f32),
            vm((3 * (height * width // 8), height * width), bf16),
            vm((WIDTH * height, width), f32),
            pltpu.SemaphoreType.DMA((11,)),
            pltpu.SemaphoreType.DMA((8, parts)),
            pltpu.SemaphoreType.DMA((8, parts)),
        ],
        compiler_params=pltpu.CompilerParams(collective_id=0, has_side_effects=True, vmem_limit_bytes=16 << 20),
    )(*(held(x) for x in (mix, diff, speed, heat, active, w1.T, w2, w3, b1[None], b2[None], b3[None])))


def solution(mesh):
    tile = P(None, "row", "col")
    plane = P("row", "col")
    return jax.shard_map(
        functools.partial(shards, mesh.shape["row"], mesh.shape["col"]),
        mesh=mesh,
        in_specs=(tile, plane, tile, plane, plane, P(), P(), P(), P(), P(), P()),
        out_specs=tile,
        check_vma=False,
    )
```

```python
import functools

import jax
import jax.numpy as jnp
from jax import lax
from jax.experimental import pallas as pl
from jax.experimental.pallas import tpu as pltpu
from jax.sharding import PartitionSpec as P

SUBSTEPS = 8
TRANSPORT_STEPS = 3
CHEM_STEP = 0.0625
GROUP = 4
SLOT = 8
CHUNKS = 2
WIDTH = 64
UNROLL = 4
PIECE = 7
MESH_ID = pl.DeviceIdType.MESH
DIRECTIONS = tuple((dr, dc) for dr in (-1, 0, 1) for dc in (-1, 0, 1) if (dr, dc) != (0, 0))


def roll_lanes(x, shift):
    return pltpu.roll(x, shift % x.shape[-1], x.ndim - 1)


def roll_rows(x, shift):
    return pltpu.roll(x, shift % x.shape[-2], x.ndim - 2)


def around_rows(centre, outer, first, last):
    cu, hu = roll_rows(centre, -1), roll_rows(outer, -1)
    cd, hd = roll_rows(centre, 1), roll_rows(outer, 1)
    return (
        jnp.where(last, hu, cu),
        jnp.where(first, hd, cd),
        jnp.where(last, cu, hu),
        jnp.where(first, cd, hd),
    )


def coefficients(d, u, v, de, dw, dn, ds, ue, uw, vn, vs):
    de, dw, dn, ds = (0.5 * (d + x) for x in (de, dw, dn, ds))
    ue, uw, vn, vs = 0.5 * (u + ue), 0.5 * (u + uw), 0.5 * (v + vn), 0.5 * (v + vs)
    own = (
        1.0
        - (de + jnp.maximum(ue, 0.0))
        - (dw - jnp.minimum(uw, 0.0))
        - (dn + jnp.maximum(vn, 0.0))
        - (ds - jnp.minimum(vs, 0.0))
    )
    return (
        own,
        de - jnp.minimum(ue, 0.0),
        dw + jnp.maximum(uw, 0.0),
        dn - jnp.minimum(vn, 0.0),
        ds + jnp.maximum(vs, 0.0),
    )


def apply_step(w, own, east, west, north, south):
    return w[0] * own + w[1] * east + w[2] * west + w[3] * north + w[4] * south


def kernel(
    rows, cols, species,
    mix_hbm, diff_hbm, speed_hbm, heat_hbm, active_hbm, w1_hbm, w2_hbm, w3_hbm,
    b1_hbm, b2_hbm, b3_hbm,
    out_ref,
    b1_ref, b2_ref, b3_ref,
    field, halo, side, corner, weight, joins, adv, heat_v, active_v, w1_v, w2_v, w3_v, w1_p, w2_p, w3_s, w3_p, b3_p, chosen, spread,
    local_sem, send_sem, recv_sem,
):
    r, c = lax.axis_index("row"), lax.axis_index("col")
    padded = pl.cdiv(species, GROUP) * GROUP
    slots = padded // GROUP
    coef = padded
    packed = padded + GROUP

    loads = [
        pltpu.make_async_copy(mix_hbm, field.at[pl.ds(0, species)], local_sem.at[0]),
        pltpu.make_async_copy(diff_hbm, field.at[coef], local_sem.at[1]),
        pltpu.make_async_copy(speed_hbm, field.at[pl.ds(coef + 1, 2)], local_sem.at[2]),
        pltpu.make_async_copy(heat_hbm, heat_v, local_sem.at[3]),
        pltpu.make_async_copy(active_hbm, active_v, local_sem.at[4]),
        pltpu.make_async_copy(w1_hbm, w1_v, local_sem.at[5]),
        pltpu.make_async_copy(w2_hbm, w2_v, local_sem.at[6]),
        pltpu.make_async_copy(w3_hbm, w3_v, local_sem.at[7]),
        pltpu.make_async_copy(b1_hbm, b1_ref, local_sem.at[8]),
        pltpu.make_async_copy(b2_hbm, b2_ref, local_sem.at[9]),
        pltpu.make_async_copy(b3_hbm, b3_ref, local_sem.at[10]),
    ]
    for load in loads:
        load.start()
    halo[...] = jnp.zeros_like(halo)
    side[...] = jnp.zeros_like(side)
    corner[...] = jnp.zeros_like(corner)

    def there(dr, dc):
        ok = jnp.bool_(True)
        if dr:
            ok = jnp.logical_and(ok, r + dr < rows if dr > 0 else r + dr >= 0)
        if dc:
            ok = jnp.logical_and(ok, c + dc < cols if dc > 0 else c + dc >= 0)
        return ok

    barrier = pltpu.get_barrier_semaphore()
    for dr, dc in DIRECTIONS:
        @pl.when(there(dr, dc))
        def _(dr=dr, dc=dc):
            pl.semaphore_signal(barrier, inc=1, device_id=(r + dr, c + dc), device_id_type=MESH_ID)

    for s in [*range(species, padded), coef + 3]:
        field[s] = jnp.zeros(field.shape[1:], jnp.float32)
    lane = lax.broadcasted_iota(jnp.int32, (8, 128), 1)
    row = lax.broadcasted_iota(jnp.int32, (8, 128), 0)
    first, last = row == 0, row == 7
    west_end, east_end = lane == 0, lane == 127
    in_slot = lane % SLOT
    slot = lane // SLOT
    for load in loads[:3]:
        load.wait()
    pack = jnp.zeros((GROUP, 8, 128), jnp.float32)
    for k in range(slots + 1):
        pack = jnp.where(slot == k, roll_lanes(field[pl.ds(GROUP * k, GROUP)], SLOT * k + 3), pack)
    field[pl.ds(packed, GROUP)] = pack

    one = lambda ok: jnp.where(ok, 1, 0)
    row_sides, col_sides = one(r > 0) + one(r < rows - 1), one(c > 0) + one(c < cols - 1)
    pl.semaphore_wait(barrier, (1 + row_sides) * (1 + col_sides) - 1)

    pieces = [(packed - GROUP, 2 * GROUP)] + [
        (GROUP * k, GROUP * min(PIECE, slots - k)) for k in range(0, slots, PIECE)
    ]

    def message(index, piece=0):
        dr, dc = DIRECTIONS[index]
        number = index if piece == 0 else 6 + 2 * piece + (dr + 1) // 2
        strip = {1: pl.ds(5, 3), -1: pl.ds(0, 3), 0: pl.ds(0, 8)}[dr]
        if dc == 0:
            some = pl.ds(*pieces[piece])
            src, dst = field.at[some, strip, :], halo.at[some, strip, :]
        else:
            target = side if dr == 0 else corner
            src = field.at[pl.ds(packed, GROUP), strip, :]
            dst = target.at[pl.ds(0 if dc > 0 else GROUP, GROUP), strip, :]
        return pltpu.make_async_remote_copy(
            src_ref=src, dst_ref=dst, send_sem=send_sem.at[number], recv_sem=recv_sem.at[number],
            device_id=(r + dr, c + dc), device_id_type=MESH_ID,
        )

    def for_each(action, numbers, sign):
        for number in numbers:
            for index, (dr, dc) in enumerate(DIRECTIONS):
                if number and dc:
                    continue

                @pl.when(there(sign * dr, sign * dc))
                def _(index=index, number=number):
                    action(message(index, number))

    def arrive(begin):
        for_each(lambda m: m.wait_recv(), [1 + begin // PIECE], -1)

    everything = range(len(pieces))
    for_each(lambda m: m.start(), everything, 1)

    for load in loads[3:]:
        load.wait()
    w1_p[...] = jnp.zeros_like(w1_p)
    w1_p[pl.ds(0, species + 1), :] = w1_v[...]
    rest = b1_ref[...]
    for i in range(3):
        term = rest.astype(jnp.bfloat16)
        w1_p[pl.ds(species + 1 + i, 1), :] = term
        rest = rest - term.astype(jnp.float32)
    w2_p[...] = jnp.transpose(w2_v[...].astype(jnp.float32)).astype(jnp.bfloat16)
    w3_s[...] = jnp.zeros_like(w3_s)
    w3_s[pl.ds(0, species), :] = w3_v[...]
    w3_p[...] = jnp.transpose(CHEM_STEP * w3_s[...].astype(jnp.float32)).astype(jnp.bfloat16)
    b3_p[...] = jnp.zeros_like(b3_p)
    b3_p[:, pl.ds(0, species)] = CHEM_STEP * b3_ref[...]

    capacity = chosen.shape[0]
    flags = jnp.where(active_v[...] == 1, 1.0, 0.0)
    upto = lax.broadcasted_iota(jnp.int32, (128, 128), 0) <= lax.broadcasted_iota(jnp.int32, (128, 128), 1)
    upto = jnp.where(upto, 1.0, 0.0).astype(jnp.bfloat16)
    within = jnp.dot(flags.astype(jnp.bfloat16), upto, preferred_element_type=jnp.float32)
    offset = jnp.dot(flags.astype(jnp.bfloat16), jnp.ones((128, 128), jnp.bfloat16), preferred_element_type=jnp.float32)
    offset = jnp.where(row >= 1, roll_rows(offset, 1), 0.0)
    for shift in (1, 2, 4):
        offset = offset + jnp.where(row >= shift, roll_rows(offset, shift), 0.0)
    place = jnp.where(flags > 0.0, within + offset - 1.0, -1.0)
    index = lax.broadcasted_iota(jnp.int32, (capacity, 128), 0).astype(jnp.float32)
    for q in range(8):
        hit = index == place[q : q + 1]
        chosen[:, 128 * q : 128 * (q + 1)] = jnp.where(hit, 1.0, 0.0).astype(jnp.bfloat16)

    for_each(lambda m: m.wait_recv(), [0], -1)

    own_c, own_h = field[pl.ds(packed, GROUP)], halo[pl.ds(packed, GROUP)]
    lower = in_slot < 3
    faces = [
        (jnp.where(lower, side[:GROUP], own_c), jnp.where(lower, corner[:GROUP], own_h)),
        (jnp.where(lower, own_c, side[GROUP:]), jnp.where(lower, own_h, corner[GROUP:])),
    ]
    in_outer = jnp.where(row < 4, jnp.where(r < rows - 1, 1.0, 0.0), jnp.where(r > 0, 1.0, 0.0))
    in_left = jnp.where(lower, jnp.where(c > 0, 1.0, 0.0), 1.0)
    in_right = jnp.where(lower, 1.0, jnp.where(c < cols - 1, 1.0, 0.0))

    def joined(left, right):
        return jnp.where(in_slot == 7, roll_lanes(right, -4), roll_lanes(left, -2))

    def around_lanes(x, join, k):
        moved = roll_lanes(join, -SLOT * k)
        return jnp.where(east_end, moved, roll_lanes(x, -1)), jnp.where(west_end, moved, roll_lanes(x, 1))

    def replicate(x):
        x = jnp.where(slot == slots, x, 0.0)
        for step in (8, 16, 32, 64):
            x = x + roll_lanes(x, step)
        return x

    def weights(dc_, uc, vc, dh, uh, vh, lanes_c, lanes_h, mask_c, mask_h):
        dnc, dsc, dnh, dsh = around_rows(dc_, dh, first, last)
        vnc, vsc, vnh, vsh = around_rows(vc, vh, first, last)
        (dec, dwc), (uec, uwc) = lanes_c
        (deh, dwh), (ueh, uwh) = lanes_h
        wc = coefficients(dc_, uc, vc, dec, dwc, dnc, dsc, uec, uwc, vnc, vsc)
        wh = coefficients(dh, uh, vh, deh, dwh, dnh, dsh, ueh, uwh, vnh, vsh)
        if mask_c is not None:
            wc = tuple(w * mask_c for w in wc)
        return wc, tuple(w * mask_h for w in wh)

    face_w = []
    for (fc, fh), mask in zip(faces, (in_left, in_right)):
        dc_, uc, vc = (replicate(fc[i]) for i in range(3))
        dh, uh, vh = (replicate(fh[i]) for i in range(3))
        pair = lambda x: (roll_lanes(x, -1), roll_lanes(x, 1))
        face_w.append(weights(dc_, uc, vc, dh, uh, vh, (pair(dc_), pair(uc)), (pair(dh), pair(uh)), mask, mask * in_outer))
    join_c, join_h = joined(faces[0][0], faces[1][0]), joined(faces[0][1], faces[1][1])
    tile_c, tile_h = field[pl.ds(coef, 3)], halo[pl.ds(coef, 3)]
    lanes_c = tuple(around_lanes(tile_c[i], join_c[i], slots) for i in range(2))
    lanes_h = tuple(around_lanes(tile_h[i], join_h[i], slots) for i in range(2))
    wc, wh = weights(*(tile_c[i] for i in range(3)), *(tile_h[i] for i in range(3)), lanes_c, lanes_h, None, in_outer)

    for i in range(5):
        weight[i] = wc[i]
        weight[5 + i] = wh[i]
    for step in range(TRANSPORT_STEPS):
        joins[2 * step] = joined(faces[0][0], faces[1][0])
        joins[2 * step + 1] = joined(faces[0][1], faces[1][1])
        if step < TRANSPORT_STEPS - 1:
            moved = []
            for (fc, fh), (fwc, fwh) in zip(faces, face_w):
                nc, sc, nh, sh = around_rows(fc, fh, first, last)
                moved.append((
                    apply_step(fwc, fc, roll_lanes(fc, -1), roll_lanes(fc, 1), nc, sc),
                    apply_step(fwh, fh, roll_lanes(fh, -1), roll_lanes(fh, 1), nh, sh),
                ))
            faces = moved

    def advance_group(k):
        here = pl.ds(GROUP * k, GROUP)
        xc, xh = field[here], halo[here]
        for step in range(TRANSPORT_STEPS):
            nc, sc, nh, sh = around_rows(xc, xh, first, last)
            ec, wcc = around_lanes(xc, joins[2 * step], k)
            new = apply_step([weight[i] for i in range(5)], xc, ec, wcc, nc, sc)
            if step < TRANSPORT_STEPS - 1:
                eh, whh = around_lanes(xh, joins[2 * step + 1], k)
                xh = apply_step([weight[5 + i] for i in range(5)], xh, eh, whh, nh, sh)
            xc = new
        adv[pl.ds(8 * GROUP * k, 8 * GROUP), :] = xc.reshape(8 * GROUP, 128)

    for begin in range(0, slots, PIECE):
        arrive(begin)
        for k in range(begin, min(begin + PIECE, slots)):
            advance_group(k)

    adv[pl.ds(8 * species, 8), :] = heat_v[...]
    adv[pl.ds(8 * (species + 1), 24), :] = jnp.ones((24, 128), jnp.float32)
    adv[pl.ds(8 * (species + 4), 8 * (WIDTH - species - 4)), :] = jnp.zeros((8 * (WIDTH - species - 4), 128), jnp.float32)
    gathered = None
    for p in range(4):
        x = jnp.concatenate([adv[pl.ds(2 * p + j, WIDTH, stride=8), :] for j in range(2)], axis=1)
        terms = []
        for _ in range(3):
            terms.append(x.astype(jnp.bfloat16))
            x = x - terms[-1].astype(jnp.float32)
        part = lax.dot_general(
            chosen[:, 256 * p : 256 * (p + 1)], jnp.concatenate(terms, axis=0),
            (((1,), (1,)), ((), ())), preferred_element_type=jnp.float32,
        )
        gathered = part if gathered is None else gathered + part
    low = jnp.concatenate([gathered[:, 128:], jnp.zeros((capacity, WIDTH), jnp.float32)], axis=1)
    state = gathered[:, :128] + roll_lanes(gathered[:, :128], WIDTH) + low
    chunk = capacity // CHUNKS
    bases = [state[chunk * i : chunk * (i + 1)] for i in range(CHUNKS)]
    bias2, bias3 = b2_ref[...], b3_p[...]

    def substep(_, states):
        hs = [jnp.dot(x.astype(jnp.bfloat16), w1_p[...], preferred_element_type=jnp.float32) for x in states]
        hs = [jnp.tanh(h).astype(jnp.bfloat16) for h in hs]
        hs = [jnp.dot(h, w2_p[...], preferred_element_type=jnp.float32) for h in hs]
        hs = [jnp.tanh(h + bias2).astype(jnp.bfloat16) for h in hs]
        hs = [jnp.dot(h, w3_p[...], preferred_element_type=jnp.float32) for h in hs]
        return tuple(x + (h + bias3) for x, h in zip(states, hs))

    states = lax.fori_loop(0, SUBSTEPS, substep, tuple(bases), unroll=UNROLL)
    total = jnp.transpose(jnp.concatenate([x - base for x, base in zip(states, bases)], axis=0))[:WIDTH]
    high = total.astype(jnp.bfloat16)
    low = (total - high.astype(jnp.float32)).astype(jnp.bfloat16)
    both = jnp.concatenate([high, low], axis=0)
    for p in range(4):
        part = jnp.dot(both, chosen[:, 256 * p : 256 * (p + 1)], preferred_element_type=jnp.float32)
        part = part[:WIDTH] + part[WIDTH:]
        for j in range(2):
            spread[pl.ds(WIDTH * (2 * p + j), WIDTH), :] = part[:, 128 * j : 128 * (j + 1)]
    for s in range(species):
        out_ref[s] = adv[pl.ds(8 * s, 8), :] + spread[pl.ds(s, 8, stride=WIDTH), :]

    for_each(lambda m: m.wait_send(), everything, 1)


def shards(rows, cols, mix, diff, speed, heat, active, w1, b1, w2, b2, w3, b3):
    species, height, width = mix.shape
    padded = pl.cdiv(species, GROUP) * GROUP
    fields = padded + 2 * GROUP
    hidden, features = w1.shape
    parts = 1 + pl.cdiv(padded // GROUP, PIECE)
    vm = pltpu.VMEM
    f32, bf16 = jnp.float32, jnp.bfloat16
    held = lambda x: pltpu.with_memory_space_constraint(x, pltpu.HBM)
    return pl.pallas_call(
        functools.partial(kernel, rows, cols, species),
        out_shape=jax.ShapeDtypeStruct(mix.shape, mix.dtype),
        in_specs=[pl.BlockSpec(memory_space=pltpu.HBM)] * 11,
        out_specs=pl.BlockSpec(memory_space=vm),
        scratch_shapes=[
            vm((1, hidden), f32),
            vm((1, hidden), f32),
            vm((1, species), f32),
            vm((fields, height, width), f32),
            vm((fields, height, width), f32),
            vm((2 * GROUP, height, width), f32),
            vm((2 * GROUP, height, width), f32),
            vm((10, height, width), f32),
            vm((2 * TRANSPORT_STEPS, GROUP, height, width), f32),
            vm((WIDTH * height, width), f32),
            vm((height, width), f32),
            vm((height, width), jnp.int32),
            vm((features, hidden), bf16),
            vm(w2.shape, bf16),
            vm(w3.shape, bf16),
            vm((128, hidden), bf16),
            vm((hidden, hidden), bf16),
            vm((128, hidden), bf16),
            vm((hidden, 128), bf16),
            vm((1, 128), f32),
            vm((3 * (height * width // 8), height * width), bf16),
            vm((WIDTH * height, width), f32),
            pltpu.SemaphoreType.DMA((11,)),
            pltpu.SemaphoreType.DMA((6 + 2 * parts,)),
            pltpu.SemaphoreType.DMA((6 + 2 * parts,)),
        ],
        compiler_params=pltpu.CompilerParams(collective_id=0, has_side_effects=True, vmem_limit_bytes=16 << 20),
    )(*(held(x) for x in (mix, diff, speed, heat, active, w1.T, w2, w3, b1[None], b2[None], b3[None])))


def solution(mesh):
    tile = P(None, "row", "col")
    plane = P("row", "col")
    return jax.shard_map(
        functools.partial(shards, mesh.shape["row"], mesh.shape["col"]),
        mesh=mesh,
        in_specs=(tile, plane, tile, plane, plane, P(), P(), P(), P(), P(), P()),
        out_specs=tile,
        check_vma=False,
    )
```
